32 devices in a mesh: chain: 8 (over z, core), bond: 4 (over y, x).
Axes of the slice: x: 2, y: 2, z: 4, core: 2. Of those that a mesh axis runs over, the one named last changes fastest.
Arguments:
- sites: bfloat16 [8, 1024, 2048], P('chain', 'bond'), may hold values from -0.1875 to 0.1875
- start: bfloat16 [8, 1024, 1024], P('chain', 'bond'), may hold values from -0.125 to 0.125
- gates: float32 [8, 16], replicated, may hold values from -3 to 3
- bonds: int32 [9], replicated, may hold values from 512 to 1024, as said below
Outputs:
- new_sites: float32 [8, 1024, 2048], P('chain', 'bond')
The draws below stay inside these ranges and needn't reach their ends.
Inputs may be any that keep to these rules, and one draw needn't show every extreme that they name: bonds[k] is the bond dimension of the cut just left of site k.
All inputs are finite; a program needn't handle non-finite values.
Results may differ from the reference program's by a relative error of at most 0.03.
Values may be sent and summed in bfloat16 or wider, within the bound.
A program may use at most 128 MiB of HBM per device.

```python
import jax
import jax.numpy as jnp
from jax import lax

CHI = 1024
SITES = 8
N_BOND = 4


def draw_bonds(key, part):
    values = jax.random.randint(key, (SITES + 1,), CHI // 2, CHI + 1).astype(jnp.int32)
    values = values.at[0].set(CHI // 2)
    return values.at[SITES // 2].set(CHI)


def levels(key, shape, shards, smallest, top_value):
    factor_of, own = 1.0, jax.random.fold_in(key, 6)
    for position, parts in shards:
        heights = jnp.exp(jax.random.uniform(jax.random.fold_in(own, position), (parts,), jnp.float32, smallest / len(shards), top_value / len(shards)))
        factor_of = factor_of * jnp.repeat(heights, shape[position] // parts).reshape([-1 if axis == position else 1 for axis in range(len(shape))])
    return factor_of


def noise(key, dims, width, limit, cuts=(), held_as=jnp.bfloat16):
    drawn = jax.random.normal(key, dims, jnp.float32) * width
    if len(cuts) > 0:
        drawn = levels(key, dims, cuts, -0.22, 0.18) * drawn
    return jnp.clip(drawn, min=-limit, max=limit).astype(held_as)


def setup_inputs(seed: int = 0) -> dict:
    key_of = jax.random.split(jax.random.key(seed), 5)
    return {
        "sites": noise(key_of[0], (SITES, CHI, 2 * CHI), CHI ** -0.5, 0.1875, ((0, 8), (1, 4))),
        "start": noise(key_of[1], (SITES, CHI, CHI), (2 * CHI) ** -0.5, 0.125, ((0, 8), (1, 4))),
        "gates": noise(key_of[2], (SITES, 16), 0.5, 3.0, (), jnp.float32),
        "bonds": draw_bonds(jax.random.fold_in(key_of[4], 71), 0),
    }


ridge_ratio = 0.05

def pair_update(left_tensor, right_tensor, start_low, start_high, gate_row, bond_left, bond_mid, bond_right):
    columns = jnp.arange(CHI)
    mid_keep = columns < bond_mid
    right_keep = columns < bond_right
    left_keep = (columns < bond_left)[:, None] & jnp.tile(mid_keep, 2)[None, :]
    left_used = jnp.where(left_keep, left_tensor, jnp.zeros((), jnp.bfloat16))
    right_used = jnp.where(jnp.tile(right_keep, 2)[None, :], right_tensor, jnp.zeros((), jnp.bfloat16))
    mix_zero = jnp.dot(left_used[:, :CHI].astype(jnp.float32), right_used.astype(jnp.float32), preferred_element_type=jnp.float32)
    mix_one = jnp.dot(left_used[:, CHI:].astype(jnp.float32), right_used.astype(jnp.float32), preferred_element_type=jnp.float32)
    gate_matrix = gate_row.reshape(4, 4)
    theta_list = []
    for out_row in range(2):
        pieces = []
        for out_col in range(2):
            coeffs = gate_matrix[2 * out_row + out_col]
            pieces.append(coeffs[0] * mix_zero[:, :CHI] + coeffs[1] * mix_zero[:, CHI:] + coeffs[2] * mix_one[:, :CHI] + coeffs[3] * mix_one[:, CHI:])
        theta_list.append(jnp.concatenate(pieces, axis=1).astype(jnp.bfloat16))
    basis_start = jnp.where(mid_keep[None, :], jnp.concatenate([start_low, start_high], axis=0), jnp.zeros((), jnp.bfloat16))
    local_rows = CHI // N_BOND
    summed = jnp.zeros((2 * CHI, CHI), jnp.float32)
    for theta_rows in theta_list:
        image_rows = jnp.dot(theta_rows.astype(jnp.float32), basis_start.astype(jnp.float32), preferred_element_type=jnp.float32).astype(jnp.bfloat16)
        split_theta = theta_rows.reshape(N_BOND, local_rows, 2 * CHI).astype(jnp.float32)
        split_image = image_rows.reshape(N_BOND, local_rows, CHI).astype(jnp.float32)
        block_terms = jnp.einsum('kar,kas->krs', split_theta, split_image)
        rounded = lax.optimization_barrier(block_terms.astype(jnp.bfloat16))
        summed = summed + lax.optimization_barrier(jnp.sum(rounded.astype(jnp.float32), axis=0))
    projected = summed
    gram_matrix = lax.dot_general(projected.astype(jnp.float32), projected.astype(jnp.float32), (((0,), (0,)), ((), ())), precision=lax.Precision.HIGHEST, preferred_element_type=jnp.float32)
    trace_sum = jnp.sum(jnp.diagonal(gram_matrix))
    kept_count = jnp.sum(mid_keep.astype(jnp.float32))
    added = jnp.where(mid_keep, ridge_ratio * trace_sum / kept_count, 1.0).astype(jnp.float32)
    factor = jnp.linalg.cholesky(gram_matrix + jnp.diag(added))
    exact_basis = lax.linalg.triangular_solve(factor, projected, left_side=False, lower=True, transpose_a=True)
    basis_new = exact_basis.astype(jnp.bfloat16)
    upper_rows = jnp.concatenate([jnp.dot(theta_rows.astype(jnp.float32), basis_new.astype(jnp.float32), preferred_element_type=jnp.float32) for theta_rows in theta_list], axis=1)
    sum_squares = jnp.sum(upper_rows * upper_rows)
    mean_square = sum_squares / (2.0 * bond_left.astype(jnp.float32) * bond_mid.astype(jnp.float32)) + 1e-06
    new_left = upper_rows * lax.rsqrt(mean_square)
    new_right = jnp.sqrt(2.0 * bond_right.astype(jnp.float32)) * exact_basis.T
    return (new_left, new_right)

def reference(sites, start, gates, bonds):
    updated = jnp.zeros((SITES, CHI, 2 * CHI), jnp.float32)

    def apply_pair(current, pair_index):
        left_site = (2 * pair_index).astype(jnp.int32)
        new_left, new_right = pair_update(sites[left_site], sites[left_site + 1], start[left_site], start[left_site + 1], gates[left_site], bonds[left_site], bonds[left_site + 1], bonds[left_site + 2])
        current = lax.dynamic_update_index_in_dim(current, new_left, left_site, 0)
        current = lax.dynamic_update_index_in_dim(current, new_right, (left_site + 1).astype(jnp.int32), 0)
        return (current, None)
    updated, _ = lax.scan(apply_pair, updated, jnp.arange(SITES // 2).astype(jnp.int32))
    return updated
```

```python
import jax
import jax.numpy as jnp
from jax import lax
from jax.experimental import pallas as pl
from jax.experimental.pallas import tpu as pltpu
from jax.sharding import PartitionSpec as P

ridge_ratio = 0.05
BLOCK = 128
SUB = 8


def partner(value, axis, apart):
    return lax.ppermute(value, axis, [(i, i ^ 1 << apart) for i in range(lax.axis_size(axis))])


def halves(x):
    high = x.astype(jnp.bfloat16)
    return high, (x - high.astype(jnp.float32)).astype(jnp.bfloat16)


def lane_of(x, j):
    return jnp.broadcast_to(x[:, j : j + 1], (SUB, BLOCK))


def row_of(x, j):
    return jnp.broadcast_to(x[j : j + 1, :], (SUB, BLOCK))


def eliminate(rows, first):
    lane = lax.broadcasted_iota(jnp.int32, (SUB, BLOCK), 1)
    sub = lax.broadcasted_iota(jnp.int32, (SUB, BLOCK), 0)
    rows = list(rows)
    for t in range(0, len(rows), 2):
        base = first + t * SUB
        inside = (lane >= base) & (lane < base + 2 * SUB)
        columns = (
            [lane_of(rows[t], base + j) for j in range(SUB)],
            [lane_of(rows[t + 1], base + j) for j in range(2 * SUB)],
        )
        below = range(t + 2, len(rows))
        held = {i: [lane_of(rows[i], base + j) for j in range(2 * SUB)] for i in below}
        current = [
            jnp.where(inside, jnp.where(lane == base + sub + h * SUB, 1.0, 0.0), rows[t + h]) for h in range(2)
        ]
        fresh = {i: jnp.where(inside, 0.0, rows[i]) for i in below}
        pivots = [jnp.ones((SUB, BLOCK), jnp.float32)] * 2
        for j in range(0, 2 * SUB, 2):
            half, local = j // SUB, j % SUB
            source = columns[half]
            a, b, c = row_of(source[j], local), row_of(source[j], local + 1), row_of(source[j + 1], local + 1)
            inverses = [1.0 / a, a * (1.0 / (a * c - b * b))]
            values = [a, c - b * b * inverses[0]]
            for q in (j, j + 1):
                inv, at = inverses[q - j], q % SUB
                pivots[half] = jnp.where(sub == at, values[q - j], pivots[half])
                uppers = {k: row_of(columns[k // SUB][q], k % SUB) for k in range(q + 1, 2 * SUB)}
                row = row_of(current[half], at)
                for h in range(half, 2):
                    m = columns[h][q] * inv
                    for k in range(q + 1, (h + 1) * SUB):
                        columns[h][k] = columns[h][k] - m * uppers[k]
                    current[h] = current[h] - (jnp.where(sub > at, m, 0.0) if h == half else m) * row
                for i in below:
                    m = held[i][q] * inv
                    for k in range(q + 1, 2 * SUB):
                        held[i][k] = held[i][k] - m * uppers[k]
                    fresh[i] = fresh[i] - m * row
        for h in range(2):
            rows[t + h] = current[h] * lax.rsqrt(pivots[h])
        for i in below:
            rows[i] = fresh[i]
    return rows


def threefold(x):
    high, low = halves(x)
    return jnp.concatenate([high, low, high], axis=0)


def threewide(x):
    high, low = halves(x)
    return jnp.concatenate([high, high, low], axis=1)


GROUP = 64


def diagonal_inverse(tile):
    part = GROUP // SUB
    rows = [tile[i * SUB : (i + 1) * SUB, :] for i in range(BLOCK // SUB)]
    for g in range(0, len(rows), part):
        rows[g : g + part] = eliminate(rows[g : g + part], g * SUB)
        if g + part < len(rows):
            done = jnp.concatenate(rows[g : g + part], axis=0)
            line = lax.broadcasted_iota(jnp.int32, done.shape, 0) + g * SUB
            lane = lax.broadcasted_iota(jnp.int32, done.shape, 1)
            right = jnp.where((lane > line) & (lane < (g + part) * SUB), 0.0, done)
            left = done.T[(g + part) * SUB :, :]
            update = jnp.dot(threewide(left), threefold(right), preferred_element_type=jnp.float32)
            lane = lax.broadcasted_iota(jnp.int32, (SUB, BLOCK), 1)
            inside = (lane >= g * SUB) & (lane < (g + part) * SUB)
            for i in range(g + part, len(rows)):
                there = slice((i - g - part) * SUB, (i - g - part + 1) * SUB)
                rows[i] = jnp.where(inside, 0.0, rows[i]) - update[there, :]
    whole = jnp.concatenate(rows, axis=0)
    line = lax.broadcasted_iota(jnp.int32, whole.shape, 0)
    lane = lax.broadcasted_iota(jnp.int32, whole.shape, 1)
    return jnp.where(lane <= line, whole, 0.0)


def turned(x):
    return x.astype(jnp.float32).T.astype(x.dtype)


def factor_kernel(bounds_ref, rows_ref, out_ref, tile_ref, inverse_ref):
    size = out_ref.shape[0]
    count = size // BLOCK
    wide = 2 * BLOCK
    for i in range(size // wide):
        left = turned(rows_ref[:, i * wide : (i + 1) * wide])
        out_ref[i * wide : (i + 1) * wide, i * wide :] = jnp.dot(
            left, rows_ref[:, i * wide :], preferred_element_type=jnp.float32
        )
    across = lax.broadcasted_iota(jnp.int32, (BLOCK, BLOCK), 1)
    eye = lax.broadcasted_iota(jnp.int32, (BLOCK, BLOCK), 0) == across
    kept = bounds_ref[1]
    diagonal = jnp.zeros((BLOCK, BLOCK), jnp.float32)
    for i in range(count):
        here = slice(i * BLOCK, (i + 1) * BLOCK)
        diagonal = diagonal + jnp.where(eye, out_ref[here, here], 0.0)
    trace = jnp.sum(jnp.sum(diagonal, axis=0, keepdims=True), axis=1, keepdims=True)
    ridge = ridge_ratio * trace / jnp.full((1, 1), kept, jnp.int32).astype(jnp.float32)
    unit = 1.0 / ridge
    root = lax.rsqrt(ridge)
    for i in range(count):
        here = slice(i * BLOCK, (i + 1) * BLOCK)
        out_ref[here, here] = out_ref[here, here] + jnp.where(eye, ridge, 0.0)
    tile_ref[...] = out_ref[0:BLOCK, 0:BLOCK] * unit
    inverse_ref[...] = jnp.zeros_like(inverse_ref)

    def finish(k, live):
        here = pl.ds(pl.multiple_of(k * BLOCK, BLOCK), BLOCK)
        inverse = inverse_ref[...]
        done = jnp.dot(threewide(inverse), threefold(out_ref[here, :]), preferred_element_type=jnp.float32)
        column = lax.broadcasted_iota(jnp.int32, (BLOCK, size), 1)
        own = (column >= k * BLOCK) & (column < (k + 1) * BLOCK)
        done = jnp.where(own, jnp.concatenate([inverse] * count, axis=1), done)
        out_ref[here, :] = jnp.where(live, jnp.where(column < (k + 1) * BLOCK, done, 0.0), out_ref[here, :])
        return done, own

    def panel(k, carry):
        before = jnp.maximum(k - 1, 0)
        inverse = diagonal_inverse(tile_ref[...]) * root
        done, own = finish(before, k > 0)
        right = threefold(done)
        for i in range(1, count):
            there = slice(i * BLOCK, (i + 1) * BLOCK)
            left = threewide(done[:, there].T)
            left = jnp.where(i >= k, left, jnp.zeros((), left.dtype))
            left = jnp.where(k > 0, left, jnp.zeros((), left.dtype))
            kept_rows = jnp.where((i >= k) & (k > 0) & own, 0.0, out_ref[there, :])
            out_ref[there, :] = kept_rows - jnp.dot(left, right, preferred_element_type=jnp.float32)
        inverse_ref[...] = inverse
        here = pl.ds(pl.multiple_of(k * BLOCK, BLOCK), BLOCK)
        after = pl.ds(pl.multiple_of(jnp.minimum(k + 1, count - 1) * BLOCK, BLOCK), BLOCK)
        across_next = jnp.dot(threewide(inverse), threefold(out_ref[here, after]), preferred_element_type=jnp.float32)
        tile_ref[...] = unit * (
            out_ref[after, after]
            - jnp.dot(threewide(across_next.T), threefold(across_next), preferred_element_type=jnp.float32)
        )
        return carry

    lax.fori_loop(0, count, panel, 0)
    finish(count - 1, kept > 0)


def factor_inverse(bounds, rows):
    size = rows.shape[1]
    return pl.pallas_call(
        factor_kernel,
        out_shape=jax.ShapeDtypeStruct((size, size), jnp.float32),
        in_specs=[pl.BlockSpec(memory_space=pltpu.SMEM), pl.BlockSpec(memory_space=pltpu.VMEM)],
        out_specs=pl.BlockSpec(memory_space=pltpu.VMEM),
        scratch_shapes=[pltpu.VMEM((BLOCK, BLOCK), jnp.float32)] * 2,
    )(bounds, rows)


CHUNK = 256


def theta_kernel(gate_ref, bounds_ref, a_ref, b_ref, start_ref, theta_ref, own_ref, image_ref):
    width = start_ref.shape[1]
    height = a_ref.shape[0]
    kept_right, kept_mid, first = bounds_ref[0], bounds_ref[1], bounds_ref[2]
    lane = lax.broadcasted_iota(jnp.int32, (height, CHUNK), 1)

    def mix(c, carry):
        offset = c * CHUNK
        inside = lane + offset < kept_right
        mixed = []
        for i in range(2):
            for j in range(2):
                columns = pl.ds(pl.multiple_of(j * width + offset, CHUNK), CHUNK)
                product = jnp.dot(
                    a_ref[:, i * width : (i + 1) * width],
                    b_ref[:, columns],
                    preferred_element_type=jnp.float32,
                )
                mixed.append(jnp.where(inside, product, 0.0))
        for o in range(2):
            for q in range(2):
                row = 4 * (2 * o + q)
                value = (
                    gate_ref[row] * mixed[0]
                    + gate_ref[row + 1] * mixed[1]
                    + gate_ref[row + 2] * mixed[2]
                    + gate_ref[row + 3] * mixed[3]
                )
                columns = pl.ds(pl.multiple_of(q * width + offset, CHUNK), CHUNK)
                theta_ref[o, :, columns] = value.astype(jnp.bfloat16)
        return carry

    lax.fori_loop(0, width // CHUNK, mix, 0)

    def image(c, carry):
        columns = pl.ds(pl.multiple_of(c * CHUNK, CHUNK), CHUNK)
        total = jnp.dot(
            theta_ref[first, :, :width], start_ref[0, :, columns], preferred_element_type=jnp.float32
        ) + jnp.dot(
            theta_ref[first, :, width:], start_ref[1, :, columns], preferred_element_type=jnp.float32
        )
        image_ref[:, columns] = jnp.where(lane + c * CHUNK < kept_mid, total, 0.0).astype(jnp.bfloat16)
        return carry

    lax.fori_loop(0, width // CHUNK, image, 0)

    def term(c, carry):
        columns = pl.ds(pl.multiple_of(c * CHUNK, CHUNK), CHUNK)
        own_ref[columns, :] = jnp.dot(
            turned(theta_ref[first, :, columns]), image_ref[...], preferred_element_type=jnp.float32
        ).astype(jnp.bfloat16)
        return carry

    lax.fori_loop(0, 2 * width // CHUNK, term, 0)


def theta_terms(gate, bounds, a_used, b_full, starts):
    height, wide = a_used.shape
    width = starts.shape[2]
    return pl.pallas_call(
        theta_kernel,
        out_shape=(
            jax.ShapeDtypeStruct((2, height, wide), jnp.bfloat16),
            jax.ShapeDtypeStruct((wide, width), jnp.bfloat16),
        ),
        in_specs=[pl.BlockSpec(memory_space=pltpu.SMEM)] * 2 + [pl.BlockSpec(memory_space=pltpu.VMEM)] * 3,
        out_specs=(pl.BlockSpec(memory_space=pltpu.VMEM),) * 2,
        scratch_shapes=[pltpu.VMEM((height, width), jnp.bfloat16)],
    )(gate, bounds, a_used, b_full, starts)


MESH = pl.DeviceIdType.MESH


class Links:
    def __init__(self, send_sem, recv_sem):
        self.chain, self.me = lax.axis_index("chain"), lax.axis_index("bond")
        self.core = self.chain % 2
        self.near = self.me + 1 - 2 * (self.me % 2)
        self.far = (self.me + 2) % 4
        self.across = 3 - self.me
        self.x, self.y, self.d = (self.chain, self.near), (self.chain, self.far), (self.chain, self.across)
        self.mate = (self.chain + 1 - 2 * self.core, self.me)
        self.send_sem, self.recv_sem, self.copies = send_sem, recv_sem, []

    def greet(self, others):
        barrier = pltpu.get_barrier_semaphore()
        for other in others:
            pl.semaphore_signal(barrier, inc=1, device_id=other, device_id_type=MESH)
        pl.semaphore_wait(barrier, len(others))

    def send(self, source, target, device):
        slot = len(self.copies)
        copy = pltpu.make_async_remote_copy(
            src_ref=source,
            dst_ref=target,
            send_sem=self.send_sem.at[slot],
            recv_sem=self.recv_sem.at[slot],
            device_id=device,
            device_id_type=MESH,
        )
        copy.start()
        self.copies.append(copy)
        return copy

    def spread(self, first_own, second_own, first, second):
        s0 = self.send(second_own, second(self.me), self.x)
        f0 = self.send(first_own, first(self.me), self.y)
        f1 = self.send(first_own, first(self.me), self.x)
        s1 = self.send(second_own, second(self.me), self.y)
        f0.wait_recv()
        f2 = self.send(first(self.far), first(self.far), self.x)
        late = [self.send(first(self.far), first(self.far), self.mate)]
        s0.wait_recv()
        s2 = self.send(second(self.near), second(self.near), self.y)
        late.append(self.send(second(self.near), second(self.near), self.mate))
        f1.wait_recv()
        late.append(self.send(first(self.near), first(self.near), self.mate))
        s1.wait_recv()
        late.append(self.send(second(self.far), second(self.far), self.mate))
        f2.wait_recv()
        late.append(self.send(first(self.across), first(self.across), self.mate))
        s2.wait_recv()
        late.append(self.send(second(self.across), second(self.across), self.mate))
        for copy in late:
            copy.wait_recv()

    def drain(self):
        for copy in self.copies:
            copy.wait_send()


def gather_kernel(b_ref, s_ref, b_out, s_out, send_sem, recv_sem, local_sem):
    links = Links(send_sem, recv_sem)
    links.greet((links.x, links.y, links.mate))
    core, me = links.core, links.me
    kept_b = pltpu.make_async_copy(b_ref, b_out.at[me], local_sem.at[0])
    kept_s = pltpu.make_async_copy(s_ref, s_out.at[core, me], local_sem.at[1])
    own = links.send(s_ref, s_out.at[core, me], links.mate)
    kept_b.start()
    kept_s.start()
    links.spread(
        b_ref.at[core], s_ref, lambda i: b_out.at[i, core], lambda i: s_out.at[core, i]
    )
    own.wait_recv()
    links.drain()
    kept_b.wait()
    kept_s.wait()


def gather_pair(b_rows, own_start):
    rows, wide = b_rows.shape
    width = own_start.shape[1]
    n = lax.axis_size("bond")
    b_full, starts = pl.pallas_call(
        gather_kernel,
        out_shape=(
            jax.ShapeDtypeStruct((n, 2, rows // 2, wide), b_rows.dtype),
            jax.ShapeDtypeStruct((2, n, rows, width), own_start.dtype),
        ),
        in_specs=[pl.BlockSpec(memory_space=pltpu.VMEM)] * 2,
        out_specs=(pl.BlockSpec(memory_space=pl.ANY),) * 2,
        scratch_shapes=[
            pltpu.SemaphoreType.DMA((13,)),
            pltpu.SemaphoreType.DMA((13,)),
            pltpu.SemaphoreType.DMA((2,)),
        ],
        compiler_params=pltpu.CompilerParams(collective_id=0, has_side_effects=True),
    )(b_rows.reshape(2, rows // 2, wide), own_start)
    return b_full.reshape(n * rows, wide), starts.reshape(2, n * rows, width)


def reduce_kernel(own_ref, out_ref, inc, acc, one, two, send_sem, recv_sem):
    links = Links(send_sem, recv_sem)
    links.greet((links.x, links.y, links.mate))
    core, me, near, far, across = links.core, links.me, links.near, links.far, links.across
    half = own_ref.shape[2] // 2
    low, high = pl.ds(0, half), pl.ds(half, half)
    order = (across, near, far, me)
    swaps = [links.send(own_ref.at[1 - core, i], inc.at[i], links.mate) for i in order]

    def merge(position):
        i = order[position]
        swaps[position].wait_recv()
        acc[i] = (own_ref[core, i].astype(jnp.float32) + inc[i].astype(jnp.float32)).astype(jnp.bfloat16)

    merge(0)
    x1 = links.send(acc.at[across, low], one.at[0, 1], links.x)
    y1 = links.send(acc.at[across, high], one.at[1, 1], links.y)
    merge(1)
    x0 = links.send(acc.at[near, low], one.at[0, 0], links.x)
    merge(2)
    y0 = links.send(acc.at[far, high], one.at[1, 0], links.y)
    merge(3)
    x1.wait_recv()
    two[2] = (acc[far, low].astype(jnp.float32) + one[0, 1].astype(jnp.float32)).astype(jnp.bfloat16)
    y2 = links.send(two.at[2], two.at[0], links.y)
    y1.wait_recv()
    two[3] = (acc[near, high].astype(jnp.float32) + one[1, 1].astype(jnp.float32)).astype(jnp.bfloat16)
    x2 = links.send(two.at[3], two.at[1], links.x)
    x0.wait_recv()
    y2.wait_recv()
    out_ref[core, me, low] = (
        acc[me, low].astype(jnp.float32) + one[0, 0].astype(jnp.float32) + two[0].astype(jnp.float32)
    ).astype(jnp.bfloat16)
    y0.wait_recv()
    x2.wait_recv()
    out_ref[core, me, high] = (
        acc[me, high].astype(jnp.float32) + one[1, 0].astype(jnp.float32) + two[1].astype(jnp.float32)
    ).astype(jnp.bfloat16)
    own = links.send(out_ref.at[core, me], out_ref.at[core, me], links.mate)
    links.spread(
        out_ref.at[core, me, low],
        out_ref.at[core, me, high],
        lambda i: out_ref.at[core, i, low],
        lambda i: out_ref.at[core, i, high],
    )
    own.wait_recv()
    links.drain()


def reduce_pair(own):
    total, width = own.shape
    n = lax.axis_size("bond")
    rows = total // (2 * n)
    whole = pl.pallas_call(
        reduce_kernel,
        out_shape=jax.ShapeDtypeStruct((2, n, rows, width), own.dtype),
        in_specs=[pl.BlockSpec(memory_space=pltpu.VMEM)],
        out_specs=pl.BlockSpec(memory_space=pltpu.VMEM),
        scratch_shapes=[
            pltpu.VMEM((n, rows, width), own.dtype),
            pltpu.VMEM((n, rows, width), own.dtype),
            pltpu.VMEM((2, 2, rows // 2, width), own.dtype),
            pltpu.VMEM((4, rows // 2, width), own.dtype),
            pltpu.SemaphoreType.DMA((23,)),
            pltpu.SemaphoreType.DMA((23,)),
        ],
        compiler_params=pltpu.CompilerParams(collective_id=1, has_side_effects=True),
    )(own.reshape(2, n, rows, width))
    return whole.reshape(total, width)


def total_kernel(value_ref, out_ref, held, send_sem, recv_sem):
    links = Links(send_sem, recv_sem)
    others = (links.x, links.y, links.d)
    links.greet(others)
    copies = [links.send(value_ref, held.at[i], other) for i, other in enumerate(others)]
    for copy in copies:
        copy.wait_recv()
    out_ref[...] = (value_ref[...] + held[2]) + (held[0] + held[1])
    links.drain()


def total_of(value):
    shape = (8, 128)
    return pl.pallas_call(
        total_kernel,
        out_shape=jax.ShapeDtypeStruct(shape, jnp.float32),
        in_specs=[pl.BlockSpec(memory_space=pltpu.VMEM)],
        out_specs=pl.BlockSpec(memory_space=pltpu.VMEM),
        scratch_shapes=[
            pltpu.VMEM((3,) + shape, jnp.float32),
            pltpu.SemaphoreType.DMA((3,)),
            pltpu.SemaphoreType.DMA((3,)),
        ],
        compiler_params=pltpu.CompilerParams(collective_id=2, has_side_effects=True),
    )(jnp.full(shape, value, jnp.float32))[:1, :1]


def local(sites, start, gates, bonds):
    bond_index = lax.axis_index("bond")
    chain_index = lax.axis_index("chain")
    rank_width = start.shape[2]
    local_rows = sites.shape[1]
    own_site = sites[0]
    own_start = start[0]
    is_left = chain_index % 2 == 0
    left_site = jnp.where(is_left, chain_index, chain_index - 1)
    bond_left = bonds[left_site]
    bond_mid = bonds[left_site + 1]
    bond_right = bonds[left_site + 2]
    columns = jnp.arange(rank_width)
    row_global = bond_index * local_rows + jnp.arange(local_rows)
    mid_keep = columns < bond_mid
    other_rows = partner(own_site, "chain", 0)
    a_rows = jnp.where(is_left, own_site, other_rows)
    b_rows = jnp.where(is_left, other_rows, own_site)
    square = lax.axis_size("bond") == 4
    if square:
        b_full, starts = gather_pair(b_rows, own_start)
    else:
        b_full = lax.all_gather(b_rows, "bond", axis=0, tiled=True)
        whole_start = lax.all_gather(own_start, "bond", axis=0, tiled=True)
        other_start = partner(whole_start, "chain", 0)
        starts = jnp.stack(
            [jnp.where(is_left, whole_start, other_start), jnp.where(is_left, other_start, whole_start)]
        )
    left_keep = (row_global < bond_left)[:, None] & jnp.tile(mid_keep, 2)[None, :]
    left_used = jnp.where(left_keep, a_rows, jnp.zeros((), jnp.bfloat16))
    bounds = jnp.stack([bond_right, bond_mid, jnp.where(is_left, 0, 1)]).astype(jnp.int32)
    thetas, own = theta_terms(gates[left_site], bounds, left_used, b_full, starts)
    if square:
        projected_all = reduce_pair(own)
    else:
        kept_half = jnp.where(is_left, 0, 1)
        half_rows = own.shape[0] // 2
        kept = lax.dynamic_slice_in_dim(own, kept_half * half_rows, half_rows, 0)
        given = lax.dynamic_slice_in_dim(own, (1 - kept_half) * half_rows, half_rows, 0)
        both = (kept.astype(jnp.float32) + partner(given, "chain", 0).astype(jnp.float32)).astype(jnp.bfloat16)
        summed = lax.psum_scatter(both, "bond", scatter_dimension=0, tiled=True)
        own_half = lax.all_gather(summed, "bond", axis=0, tiled=True)
        other_half = partner(own_half, "chain", 0)
        projected_all = jnp.concatenate(
            [jnp.where(is_left, own_half, other_half), jnp.where(is_left, other_half, own_half)], axis=0
        )
    inverse = factor_inverse(bounds, projected_all)

    def left_rows():
        reduced = jnp.dot(
            thetas.reshape(2 * local_rows, -1), projected_all, preferred_element_type=jnp.float32
        )
        upper = lax.dot_general(
            reduced,
            inverse,
            (((1,), (1,)), ((), ())),
            precision=lax.Precision.HIGH,
            preferred_element_type=jnp.float32,
        )
        joined = jnp.concatenate([upper[:local_rows], upper[local_rows:]], axis=1)
        return joined, jnp.sum(joined * joined)

    def right_rows():
        block = lax.dynamic_slice_in_dim(inverse, bond_index * local_rows, local_rows, 0)
        basis_rows = lax.dot_general(
            block,
            projected_all.astype(jnp.float32),
            (((1,), (1,)), ((), ())),
            precision=lax.Precision.HIGH,
            preferred_element_type=jnp.float32,
        )
        return basis_rows, jnp.float32(0.0)

    rows, squares = lax.cond(is_left, left_rows, right_rows)
    sum_squares = total_of(squares) if square else lax.psum(squares, "bond")
    mean_square = (
        sum_squares / (2.0 * bond_left.astype(jnp.float32) * bond_mid.astype(jnp.float32)) + 1e-06
    )
    factor = jnp.where(
        jnp.full(jnp.shape(mean_square), is_left), lax.rsqrt(mean_square), jnp.sqrt(2.0 * bond_right.astype(jnp.float32))
    )
    return (rows * factor)[None]


def solution(mesh):
    placed = (P("chain", "bond", None), P("chain", "bond", None), P(), P())
    return jax.shard_map(
        local, mesh=mesh, in_specs=placed, out_specs=P("chain", "bond", None), check_vma=False
    )
```

```python
import jax
import jax.numpy as jnp
from jax import lax
from jax.experimental import pallas as pl
from jax.experimental.pallas import tpu as pltpu
from jax.sharding import PartitionSpec as P

ridge_ratio = 0.05
BLOCK = 128
SUB = 8


def partner(value, axis, apart):
    return lax.ppermute(value, axis, [(i, i ^ 1 << apart) for i in range(lax.axis_size(axis))])


def halves(x):
    high = x.astype(jnp.bfloat16)
    return high, (x - high.astype(jnp.float32)).astype(jnp.bfloat16)


def lane_of(x, j):
    return jnp.broadcast_to(x[:, j : j + 1], (SUB, BLOCK))


def row_of(x, j):
    return jnp.broadcast_to(x[j : j + 1, :], (SUB, BLOCK))


def eliminate(rows, first):
    lane = lax.broadcasted_iota(jnp.int32, (SUB, BLOCK), 1)
    sub = lax.broadcasted_iota(jnp.int32, (SUB, BLOCK), 0)
    rows = list(rows)
    for t in range(0, len(rows), 2):
        base = first + t * SUB
        inside = (lane >= base) & (lane < base + 2 * SUB)
        columns = (
            [lane_of(rows[t], base + j) for j in range(SUB)],
            [lane_of(rows[t + 1], base + j) for j in range(2 * SUB)],
        )
        below = range(t + 2, len(rows))
        held = {i: [lane_of(rows[i], base + j) for j in range(2 * SUB)] for i in below}
        current = [
            jnp.where(inside, jnp.where(lane == base + sub + h * SUB, 1.0, 0.0), rows[t + h]) for h in range(2)
        ]
        fresh = {i: jnp.where(inside, 0.0, rows[i]) for i in below}
        pivots = [jnp.ones((SUB, BLOCK), jnp.float32)] * 2
        for j in range(0, 2 * SUB, 2):
            half, local = j // SUB, j % SUB
            source = columns[half]
            a, b, c = row_of(source[j], local), row_of(source[j], local + 1), row_of(source[j + 1], local + 1)
            inverses = [1.0 / a, a * (1.0 / (a * c - b * b))]
            values = [a, c - b * b * inverses[0]]
            for q in (j, j + 1):
                inv, at = inverses[q - j], q % SUB
                pivots[half] = jnp.where(sub == at, values[q - j], pivots[half])
                uppers = {k: row_of(columns[k // SUB][q], k % SUB) for k in range(q + 1, 2 * SUB)}
                row = row_of(current[half], at)
                for h in range(half, 2):
                    m = columns[h][q] * inv
                    for k in range(q + 1, (h + 1) * SUB):
                        columns[h][k] = columns[h][k] - m * uppers[k]
                    current[h] = current[h] - (jnp.where(sub > at, m, 0.0) if h == half else m) * row
                for i in below:
                    m = held[i][q] * inv
                    for k in range(q + 1, 2 * SUB):
                        held[i][k] = held[i][k] - m * uppers[k]
                    fresh[i] = fresh[i] - m * row
        for h in range(2):
            rows[t + h] = current[h] * lax.rsqrt(pivots[h])
        for i in below:
            rows[i] = fresh[i]
    return rows


def threefold(x):
    high, low = halves(x)
    return jnp.concatenate([high, low, high], axis=0)


def threewide(x):
    high, low = halves(x)
    return jnp.concatenate([high, high, low], axis=1)


GROUP = 64


def diagonal_inverse(tile):
    part = GROUP // SUB
    rows = [tile[i * SUB : (i + 1) * SUB, :] for i in range(BLOCK // SUB)]
    for g in range(0, len(rows), part):
        rows[g : g + part] = eliminate(rows[g : g + part], g * SUB)
        if g + part < len(rows):
            done = jnp.concatenate(rows[g : g + part], axis=0)
            line = lax.broadcasted_iota(jnp.int32, done.shape, 0) + g * SUB
            lane = lax.broadcasted_iota(jnp.int32, done.shape, 1)
            right = jnp.where((lane > line) & (lane < (g + part) * SUB), 0.0, done)
            left = done.T[(g + part) * SUB :, :]
            update = jnp.dot(threewide(left), threefold(right), preferred_element_type=jnp.float32)
            lane = lax.broadcasted_iota(jnp.int32, (SUB, BLOCK), 1)
            inside = (lane >= g * SUB) & (lane < (g + part) * SUB)
            for i in range(g + part, len(rows)):
                there = slice((i - g - part) * SUB, (i - g - part + 1) * SUB)
                rows[i] = jnp.where(inside, 0.0, rows[i]) - update[there, :]
    whole = jnp.concatenate(rows, axis=0)
    line = lax.broadcasted_iota(jnp.int32, whole.shape, 0)
    lane = lax.broadcasted_iota(jnp.int32, whole.shape, 1)
    return jnp.where(lane <= line, whole, 0.0)


def turned(x):
    return x.astype(jnp.float32).T.astype(x.dtype)


def factor_kernel(bounds_ref, gram_ref, out_ref, tile_ref, inverse_ref):
    size = out_ref.shape[0]
    count = size // BLOCK
    out_ref[...] = gram_ref[...]
    across = lax.broadcasted_iota(jnp.int32, (BLOCK, BLOCK), 1)
    eye = lax.broadcasted_iota(jnp.int32, (BLOCK, BLOCK), 0) == across
    kept = bounds_ref[1]
    diagonal = jnp.zeros((BLOCK, BLOCK), jnp.float32)
    for i in range(count):
        here = slice(i * BLOCK, (i + 1) * BLOCK)
        diagonal = diagonal + jnp.where(eye, out_ref[here, here], 0.0)
    trace = jnp.sum(jnp.sum(diagonal, axis=0, keepdims=True), axis=1, keepdims=True)
    ridge = ridge_ratio * trace / jnp.full((1, 1), kept, jnp.int32).astype(jnp.float32)
    unit = 1.0 / ridge
    root = lax.rsqrt(ridge)
    for i in range(count):
        here = slice(i * BLOCK, (i + 1) * BLOCK)
        out_ref[here, here] = out_ref[here, here] + jnp.where(eye, ridge, 0.0)
    tile_ref[...] = out_ref[0:BLOCK, 0:BLOCK] * unit
    inverse_ref[...] = jnp.zeros_like(inverse_ref)

    def finish(k, live):
        here = pl.ds(pl.multiple_of(k * BLOCK, BLOCK), BLOCK)
        inverse = inverse_ref[...]
        done = jnp.dot(threewide(inverse), threefold(out_ref[here, :]), preferred_element_type=jnp.float32)
        column = lax.broadcasted_iota(jnp.int32, (BLOCK, size), 1)
        own = (column >= k * BLOCK) & (column < (k + 1) * BLOCK)
        done = jnp.where(own, jnp.concatenate([inverse] * count, axis=1), done)
        out_ref[here, :] = jnp.where(live, jnp.where(column < (k + 1) * BLOCK, done, 0.0), out_ref[here, :])
        return done, own

    def panel(k, carry):
        before = jnp.maximum(k - 1, 0)
        inverse = diagonal_inverse(tile_ref[...]) * root
        done, own = finish(before, k > 0)
        right = threefold(done)
        for i in range(1, count):
            there = slice(i * BLOCK, (i + 1) * BLOCK)
            left = threewide(done[:, there].T)
            left = jnp.where(i >= k, left, jnp.zeros((), left.dtype))
            left = jnp.where(k > 0, left, jnp.zeros((), left.dtype))
            kept_rows = jnp.where((i >= k) & (k > 0) & own, 0.0, out_ref[there, :])
            out_ref[there, :] = kept_rows - jnp.dot(left, right, preferred_element_type=jnp.float32)
        inverse_ref[...] = inverse
        here = pl.ds(pl.multiple_of(k * BLOCK, BLOCK), BLOCK)
        after = pl.ds(pl.multiple_of(jnp.minimum(k + 1, count - 1) * BLOCK, BLOCK), BLOCK)
        across_next = jnp.dot(threewide(inverse), threefold(out_ref[here, after]), preferred_element_type=jnp.float32)
        tile_ref[...] = unit * (
            out_ref[after, after]
            - jnp.dot(threewide(across_next.T), threefold(across_next), preferred_element_type=jnp.float32)
        )
        return carry

    lax.fori_loop(0, count, panel, 0)
    finish(count - 1, kept > 0)


def factor_inverse(bounds, gram):
    size = gram.shape[1]
    return pl.pallas_call(
        factor_kernel,
        out_shape=jax.ShapeDtypeStruct((size, size), jnp.float32),
        in_specs=[pl.BlockSpec(memory_space=pltpu.SMEM), pl.BlockSpec(memory_space=pltpu.VMEM)],
        out_specs=pl.BlockSpec(memory_space=pltpu.VMEM),
        scratch_shapes=[pltpu.VMEM((BLOCK, BLOCK), jnp.float32)] * 2,
    )(bounds, gram)


CHUNK = 256


def theta_kernel(gate_ref, bounds_ref, a_ref, b_ref, start_ref, theta_ref, own_ref, image_ref):
    width = start_ref.shape[1]
    height = a_ref.shape[0]
    kept_right, kept_mid, first = bounds_ref[0], bounds_ref[1], bounds_ref[2]
    lane = lax.broadcasted_iota(jnp.int32, (height, CHUNK), 1)

    def mix(c, carry):
        offset = c * CHUNK
        inside = lane + offset < kept_right
        mixed = []
        for i in range(2):
            for j in range(2):
                columns = pl.ds(pl.multiple_of(j * width + offset, CHUNK), CHUNK)
                product = jnp.dot(
                    a_ref[:, i * width : (i + 1) * width],
                    b_ref[:, columns],
                    preferred_element_type=jnp.float32,
                )
                mixed.append(jnp.where(inside, product, 0.0))
        for o in range(2):
            for q in range(2):
                row = 4 * (2 * o + q)
                value = (
                    gate_ref[row] * mixed[0]
                    + gate_ref[row + 1] * mixed[1]
                    + gate_ref[row + 2] * mixed[2]
                    + gate_ref[row + 3] * mixed[3]
                )
                columns = pl.ds(pl.multiple_of(q * width + offset, CHUNK), CHUNK)
                theta_ref[o, :, columns] = value.astype(jnp.bfloat16)
        return carry

    lax.fori_loop(0, width // CHUNK, mix, 0)

    def image(c, carry):
        columns = pl.ds(pl.multiple_of(c * CHUNK, CHUNK), CHUNK)
        total = jnp.dot(
            theta_ref[first, :, :width], start_ref[0, :, columns], preferred_element_type=jnp.float32
        ) + jnp.dot(
            theta_ref[first, :, width:], start_ref[1, :, columns], preferred_element_type=jnp.float32
        )
        image_ref[:, columns] = jnp.where(lane + c * CHUNK < kept_mid, total, 0.0).astype(jnp.bfloat16)
        return carry

    lax.fori_loop(0, width // CHUNK, image, 0)

    def term(c, carry):
        columns = pl.ds(pl.multiple_of(c * CHUNK, CHUNK), CHUNK)
        own_ref[columns, :] = jnp.dot(
            turned(theta_ref[first, :, columns]), image_ref[...], preferred_element_type=jnp.float32
        ).astype(jnp.bfloat16)
        return carry

    lax.fori_loop(0, 2 * width // CHUNK, term, 0)


def theta_terms(gate, bounds, a_used, b_full, starts):
    height, wide = a_used.shape
    width = starts.shape[2]
    return pl.pallas_call(
        theta_kernel,
        out_shape=(
            jax.ShapeDtypeStruct((2, height, wide), jnp.bfloat16),
            jax.ShapeDtypeStruct((wide, width), jnp.bfloat16),
        ),
        in_specs=[pl.BlockSpec(memory_space=pltpu.SMEM)] * 2 + [pl.BlockSpec(memory_space=pltpu.VMEM)] * 3,
        out_specs=(pl.BlockSpec(memory_space=pltpu.VMEM),) * 2,
        scratch_shapes=[pltpu.VMEM((height, width), jnp.bfloat16)],
    )(gate, bounds, a_used, b_full, starts)


MESH = pl.DeviceIdType.MESH


class Links:
    def __init__(self, send_sem, recv_sem):
        self.chain, self.me = lax.axis_index("chain"), lax.axis_index("bond")
        self.core = self.chain % 2
        self.near = self.me + 1 - 2 * (self.me % 2)
        self.far = (self.me + 2) % 4
        self.across = 3 - self.me
        self.x, self.y, self.d = (self.chain, self.near), (self.chain, self.far), (self.chain, self.across)
        self.mate = (self.chain + 1 - 2 * self.core, self.me)
        self.send_sem, self.recv_sem, self.copies = send_sem, recv_sem, []

    def greet(self, others):
        barrier = pltpu.get_barrier_semaphore()
        for other in others:
            pl.semaphore_signal(barrier, inc=1, device_id=other, device_id_type=MESH)
        pl.semaphore_wait(barrier, len(others))

    def send(self, source, target, device):
        slot = len(self.copies)
        copy = pltpu.make_async_remote_copy(
            src_ref=source,
            dst_ref=target,
            send_sem=self.send_sem.at[slot],
            recv_sem=self.recv_sem.at[slot],
            device_id=device,
            device_id_type=MESH,
        )
        copy.start()
        self.copies.append(copy)
        return copy

    def drain(self):
        for copy in self.copies:
            copy.wait_send()


def add(x, y):
    return x.astype(jnp.float32) + y.astype(jnp.float32)


def pair_kernel(
    gate_ref, bond_ref, site_ref, start_ref, theta_ref, x_ref, gram_ref,
    ab, used, b_all, s_all, mixed, image, image_t, own, inc, acc, one, two, send_sem, recv_sem, local_sem,
):
    links = Links(send_sem, recv_sem)
    links.greet((links.x, links.y, links.mate))
    core, me, near, far, across = links.core, links.me, links.near, links.far, links.across
    send = links.send
    height, wide = site_ref.shape
    width = wide // 2
    left_site = links.chain - core
    kept_left, kept_mid, kept_right = bond_ref[left_site], bond_ref[left_site + 1], bond_ref[left_site + 2]
    half = height // 2
    mine = pl.ds(pl.multiple_of(core * half, half), half)
    quarter = half // 2

    held = pltpu.make_async_copy(site_ref, ab.at[core], local_sem.at[0])
    held_start = pltpu.make_async_copy(start_ref, s_all.at[core, me], local_sem.at[1])
    held.start()
    held_start.start()
    first = send(site_ref.at[pl.ds(0, half)], ab.at[core, pl.ds(0, half)], links.mate)
    second = send(site_ref.at[pl.ds(half, half)], ab.at[core, pl.ds(half, half)], links.mate)

    def s_piece(i, p):
        return s_all.at[core, i, pl.ds(p * half, half)]

    def s_own(p):
        return start_ref.at[pl.ds(p * half, half)]

    def b_piece(i, p):
        return b_all.at[i, core, pl.ds(p * quarter, quarter)]

    def b_own(p):
        return ab.at[1, pl.ds(pl.multiple_of(core * half + p * quarter, quarter), quarter)]

    s0x = send(s_own(0), s_piece(me, 0), links.x)
    s1y = send(s_own(1), s_piece(me, 1), links.y)
    start_mate = send(start_ref, s_all.at[core, me], links.mate)
    held.wait()
    first.wait_recv()
    b0x = send(b_own(0), b_piece(me, 0), links.x)
    b1y = send(b_own(1), b_piece(me, 1), links.y)
    second.wait_recv()
    b1x = send(b_own(1), b_piece(me, 1), links.x)
    b0y = send(b_own(0), b_piece(me, 0), links.y)

    line = lax.broadcasted_iota(jnp.int32, (height, CHUNK), 0) + me * height
    lane = lax.broadcasted_iota(jnp.int32, (height, CHUNK), 1)

    def mask(c, carry):
        for i in range(2):
            columns = pl.ds(pl.multiple_of(i * width + c * CHUNK, CHUNK), CHUNK)
            keep = (line < kept_left) & (lane + c * CHUNK < kept_mid)
            used[:, columns] = jnp.where(keep, ab[0, :, columns].astype(jnp.float32), 0.0).astype(jnp.bfloat16)
        return carry

    lax.fori_loop(0, width // CHUNK, mask, 0)

    def mix(load, index, fresh):
        def step(c, carry):
            columns = pl.ds(pl.multiple_of(c * CHUNK, CHUNK), CHUNK)
            right = load(columns)
            for i in range(2):
                left = used[:, pl.ds(pl.multiple_of(i * width + index * height, height), height)]
                product = jnp.dot(left, right, preferred_element_type=jnp.float32)
                mixed[i, :, columns] = product if fresh else mixed[i, :, columns] + product
            return carry

        lax.fori_loop(0, wide // CHUNK, step, 0)

    def gathered(i):
        return lambda columns: b_all[i, :, :, columns].reshape(height, CHUNK)

    mix(lambda columns: ab[1, :, columns], me, True)

    s0x.wait_recv()
    sf_y = send(s_piece(near, 0), s_piece(near, 0), links.y)
    relay = [send(s_piece(near, 0), s_piece(near, 0), links.mate)]
    s1y.wait_recv()
    sf_x = send(s_piece(far, 1), s_piece(far, 1), links.x)
    relay.append(send(s_piece(far, 1), s_piece(far, 1), links.mate))
    b0x.wait_recv()
    bf_y = send(b_piece(near, 0), b_piece(near, 0), links.y)
    relay_b = [send(b_piece(near, 0), b_piece(near, 0), links.mate)]
    b1y.wait_recv()
    bf_x = send(b_piece(far, 1), b_piece(far, 1), links.x)
    relay_b.append(send(b_piece(far, 1), b_piece(far, 1), links.mate))
    s1x = send(s_own(1), s_piece(me, 1), links.x)
    s0y = send(s_own(0), s_piece(me, 0), links.y)
    b1x.wait_recv()
    relay_b.append(send(b_piece(near, 1), b_piece(near, 1), links.mate))
    b0y.wait_recv()
    relay_b.append(send(b_piece(far, 0), b_piece(far, 0), links.mate))
    for copy in relay_b:
        copy.wait_recv()
    mix(gathered(near), near, False)
    mix(gathered(far), far, False)
    sf_y.wait_recv()
    relay.append(send(s_piece(across, 0), s_piece(across, 0), links.mate))
    sf_x.wait_recv()
    relay.append(send(s_piece(across, 1), s_piece(across, 1), links.mate))
    bf_y.wait_recv()
    last_b = [send(b_piece(across, 0), b_piece(across, 0), links.mate)]
    bf_x.wait_recv()
    last_b.append(send(b_piece(across, 1), b_piece(across, 1), links.mate))
    for copy in last_b:
        copy.wait_recv()
    mix(gathered(across), across, False)

    def form(c, carry):
        offset = c * CHUNK
        inside = lane + offset < kept_right
        parts = []
        for i in range(2):
            for j in range(2):
                columns = pl.ds(pl.multiple_of(j * width + offset, CHUNK), CHUNK)
                parts.append(jnp.where(inside, mixed[i, :, columns], 0.0))
        for o in range(2):
            for q in range(2):
                row = 4 * (2 * o + q)
                value = (
                    gate_ref[left_site, row] * parts[0]
                    + gate_ref[left_site, row + 1] * parts[1]
                    + gate_ref[left_site, row + 2] * parts[2]
                    + gate_ref[left_site, row + 3] * parts[3]
                )
                columns = pl.ds(pl.multiple_of(q * width + offset, CHUNK), CHUNK)
                theta_ref[o, :, columns] = value.astype(jnp.bfloat16)
        return carry

    lax.fori_loop(0, width // CHUNK, form, 0)

    def apply(q, i, fresh=False):
        def step(c, carry):
            columns = pl.ds(pl.multiple_of(c * CHUNK, CHUNK), CHUNK)
            rows = pl.ds(pl.multiple_of(q * width + i * height, height), height)
            product = jnp.dot(
                theta_ref[core, :, rows], s_all[q, i, :, columns], preferred_element_type=jnp.float32
            )
            image[:, columns] = product if fresh else image[:, columns] + product
            return carry

        lax.fori_loop(0, width // CHUNK, step, 0)

    held_start.wait()
    apply(core, me, True)
    start_mate.wait_recv()
    apply(1 - core, me)
    s1x.wait_recv()
    relay.append(send(s_piece(near, 1), s_piece(near, 1), links.mate))
    s0y.wait_recv()
    relay.append(send(s_piece(far, 0), s_piece(far, 0), links.mate))
    for i in (across, near, far):
        apply(core, i)
    for copy in relay:
        copy.wait_recv()
    for i in (across, near, far):
        apply(1 - core, i)

    def turn(c, carry):
        columns = pl.ds(pl.multiple_of(c * CHUNK, CHUNK), CHUNK)
        image_t[columns, :] = jnp.where(lane + c * CHUNK < kept_mid, image[:, columns], 0.0).T.astype(jnp.bfloat16)
        return carry

    lax.fori_loop(0, width // CHUNK, turn, 0)

    def term(h, i):
        columns = pl.ds(pl.multiple_of(h * width + i * height, height), height)

        def step(c, carry):
            rows = pl.ds(pl.multiple_of(c * CHUNK, CHUNK), CHUNK)
            own[h, i, rows, :] = jnp.dot(
                image_t[rows, :], theta_ref[core, :, columns], preferred_element_type=jnp.float32
            ).astype(jnp.bfloat16)
            return carry

        lax.fori_loop(0, width // CHUNK, step, 0)

    order = (across, near, far, me)
    swaps = []
    for i in order:
        term(1 - core, i)
        swaps.append(send(own.at[1 - core, i], inc.at[i], links.mate))
    low, high = pl.ds(0, width // 2), pl.ds(width // 2, width // 2)

    def merge(position):
        i = order[position]
        term(core, i)
        swaps[position].wait_recv()
        acc[i] = add(own[core, i], inc[i]).astype(jnp.bfloat16)

    merge(0)
    x1 = send(acc.at[across, low], one.at[0, 1], links.x)
    y1 = send(acc.at[across, high], one.at[1, 1], links.y)
    merge(1)
    x0 = send(acc.at[near, low], one.at[0, 0], links.x)
    merge(2)
    y0 = send(acc.at[far, high], one.at[1, 0], links.y)
    merge(3)
    x1.wait_recv()
    two[2] = add(acc[far, low], one[0, 1]).astype(jnp.bfloat16)
    y2 = send(two.at[2], two.at[0], links.y)
    y1.wait_recv()
    two[3] = add(acc[near, high], one[1, 1]).astype(jnp.bfloat16)
    x2 = send(two.at[3], two.at[1], links.x)
    x0.wait_recv()
    y2.wait_recv()
    x_ref[core, me, low] = (add(acc[me, low], one[0, 0]) + two[0].astype(jnp.float32)).astype(jnp.bfloat16)

    def first_of(i):
        return x_ref.at[core, i, low]

    def second_of(i):
        return x_ref.at[core, i, high]

    f0 = send(first_of(me), first_of(me), links.y)
    f1 = send(first_of(me), first_of(me), links.x)
    y0.wait_recv()
    x2.wait_recv()
    x_ref[core, me, high] = (add(acc[me, high], one[1, 0]) + two[1].astype(jnp.float32)).astype(jnp.bfloat16)
    s0 = send(second_of(me), second_of(me), links.x)
    s1 = send(second_of(me), second_of(me), links.y)
    whole_mate = send(x_ref.at[core, me], x_ref.at[core, me], links.mate)

    def square(h, i, fresh=False):
        for k in range(width // CHUNK):
            rows = slice(k * CHUNK, (k + 1) * CHUNK)
            product = lax.dot_general(
                x_ref[h, i, rows, :],
                x_ref[h, i, k * CHUNK :, :],
                (((1,), (1,)), ((), ())),
                preferred_element_type=jnp.float32,
            )
            gram_ref[rows, k * CHUNK :] = product if fresh else gram_ref[rows, k * CHUNK :] + product

    square(core, me, True)
    f0.wait_recv()
    f2 = send(first_of(far), first_of(far), links.x)
    late_far = [send(first_of(far), first_of(far), links.mate)]
    s0.wait_recv()
    s2 = send(second_of(near), second_of(near), links.y)
    late_near = [send(second_of(near), second_of(near), links.mate)]
    f1.wait_recv()
    late_near.append(send(first_of(near), first_of(near), links.mate))
    s1.wait_recv()
    late_far.append(send(second_of(far), second_of(far), links.mate))
    whole_mate.wait_recv()
    square(1 - core, me)
    square(core, near)
    square(core, far)
    for copy in late_near:
        copy.wait_recv()
    square(1 - core, near)
    for copy in late_far:
        copy.wait_recv()
    square(1 - core, far)
    f2.wait_recv()
    late = [send(first_of(across), first_of(across), links.mate)]
    s2.wait_recv()
    late.append(send(second_of(across), second_of(across), links.mate))
    square(core, across)
    for copy in late:
        copy.wait_recv()
    square(1 - core, across)
    links.drain()


def pair_step(gates, bonds, own_site, own_start):
    rows, wide = own_site.shape
    width = wide // 2
    n = lax.axis_size("bond")
    kind = jnp.bfloat16
    copies = 50
    return pl.pallas_call(
        pair_kernel,
        out_shape=(
            jax.ShapeDtypeStruct((2, rows, wide), kind),
            jax.ShapeDtypeStruct((2, n, width, rows), kind),
            jax.ShapeDtypeStruct((width, width), jnp.float32),
        ),
        in_specs=[pl.BlockSpec(memory_space=pltpu.SMEM)] * 2 + [pl.BlockSpec(memory_space=pltpu.VMEM)] * 2,
        out_specs=(pl.BlockSpec(memory_space=pltpu.VMEM),) * 3,
        scratch_shapes=[
            pltpu.VMEM((2, rows, wide), kind),
            pltpu.VMEM((rows, wide), kind),
            pltpu.VMEM((n, 2, rows // 2, wide), kind),
            pltpu.VMEM((2, n, rows, width), kind),
            pltpu.VMEM((2, rows, wide), jnp.float32),
            pltpu.VMEM((rows, width), jnp.float32),
            pltpu.VMEM((width, rows), kind),
            pltpu.VMEM((2, n, width, rows), kind),
            pltpu.VMEM((n, width, rows), kind),
            pltpu.VMEM((n, width, rows), kind),
            pltpu.VMEM((2, 2, width // 2, rows), kind),
            pltpu.VMEM((4, width // 2, rows), kind),
            pltpu.SemaphoreType.DMA((copies,)),
            pltpu.SemaphoreType.DMA((copies,)),
            pltpu.SemaphoreType.DMA((2,)),
        ],
        compiler_params=pltpu.CompilerParams(
            collective_id=0, has_side_effects=True, vmem_limit_bytes=56 * 1024 * 1024
        ),
    )(gates, bonds, own_site, own_start)


def final_kernel(theta_ref, x_ref, inverse_ref, out_ref, square_ref, reduced_ref):
    core, me = lax.axis_index("chain") % 2, lax.axis_index("bond")
    n, width, rows = x_ref.shape[1:]
    nt = (((1,), (1,)), ((), ()))

    @pl.when(core == 0)
    def _():
        total = jnp.zeros((SUB, BLOCK), jnp.float32)
        for o in range(2):
            def reduce(c, carry):
                columns = pl.ds(pl.multiple_of(c * CHUNK, CHUNK), CHUNK)
                value = jnp.zeros((rows, CHUNK), jnp.float32)
                for h in range(2):
                    for i in range(n):
                        at = h * width + i * rows
                        value = value + lax.dot_general(
                            theta_ref[o, :, at : at + rows], x_ref[h, i, columns, :], nt,
                            preferred_element_type=jnp.float32,
                        )
                high, low = halves(value)
                reduced_ref[0, :, columns] = high
                reduced_ref[1, :, columns] = low
                return carry

            lax.fori_loop(0, width // CHUNK, reduce, 0)
            for c in range(width // CHUNK):
                reach = (c + 1) * CHUNK
                high, low = halves(inverse_ref[c * CHUNK : reach, :reach])
                left_high, left_low = reduced_ref[0, :, :reach], reduced_ref[1, :, :reach]
                value = lax.dot_general(
                    jnp.concatenate([left_high, left_high, left_low], axis=1),
                    jnp.concatenate([high, low, high], axis=1),
                    nt,
                    preferred_element_type=jnp.float32,
                )
                out_ref[:, o * width + c * CHUNK : o * width + reach] = value
                squared = value * value
                for j in range(CHUNK // BLOCK):
                    part = squared[:, j * BLOCK : (j + 1) * BLOCK]
                    total = total + jnp.sum(part.reshape(rows // SUB, SUB, BLOCK), axis=0)
        summed = jnp.sum(jnp.sum(total, axis=0, keepdims=True), axis=1, keepdims=True)
        square_ref[...] = jnp.broadcast_to(summed, (SUB, BLOCK))

    @pl.when(core == 1)
    def _():
        high, low = halves(inverse_ref[pl.ds(pl.multiple_of(me * rows, rows), rows), :])
        for h in range(2):
            for i in range(n):
                block = x_ref[h, i]
                at = h * width + i * rows
                out_ref[:, at : at + rows] = jnp.dot(
                    high, block, preferred_element_type=jnp.float32
                ) + jnp.dot(low, block, preferred_element_type=jnp.float32)
        square_ref[...] = jnp.zeros((SUB, BLOCK), jnp.float32)


def final_rows(thetas, x, inverse):
    rows, wide = thetas.shape[1:]
    return pl.pallas_call(
        final_kernel,
        out_shape=(
            jax.ShapeDtypeStruct((rows, wide), jnp.float32),
            jax.ShapeDtypeStruct((SUB, BLOCK), jnp.float32),
        ),
        in_specs=[pl.BlockSpec(memory_space=pltpu.VMEM)] * 3,
        out_specs=(pl.BlockSpec(memory_space=pltpu.VMEM),) * 2,
        scratch_shapes=[pltpu.VMEM((2, rows, wide // 2), jnp.bfloat16)],
        compiler_params=pltpu.CompilerParams(vmem_limit_bytes=56 * 1024 * 1024),
    )(thetas, x, inverse)


def total_kernel(value_ref, out_ref, held, send_sem, recv_sem):
    links = Links(send_sem, recv_sem)
    others = (links.x, links.y, links.d)
    links.greet(others)
    copies = [links.send(value_ref, held.at[i], other) for i, other in enumerate(others)]
    for copy in copies:
        copy.wait_recv()
    out_ref[...] = (value_ref[...] + held[2]) + (held[0] + held[1])
    links.drain()


def total_of(value):
    shape = (8, 128)
    return pl.pallas_call(
        total_kernel,
        out_shape=jax.ShapeDtypeStruct(shape, jnp.float32),
        in_specs=[pl.BlockSpec(memory_space=pltpu.VMEM)],
        out_specs=pl.BlockSpec(memory_space=pltpu.VMEM),
        scratch_shapes=[
            pltpu.VMEM((3,) + shape, jnp.float32),
            pltpu.SemaphoreType.DMA((3,)),
            pltpu.SemaphoreType.DMA((3,)),
        ],
        compiler_params=pltpu.CompilerParams(collective_id=2, has_side_effects=True),
    )(value)[:1, :1]


def scaled(rows, sum_squares, bond_left, bond_mid, bond_right, is_left):
    mean_square = (
        sum_squares / (2.0 * bond_left.astype(jnp.float32) * bond_mid.astype(jnp.float32)) + 1e-06
    )
    factor = jnp.where(
        jnp.full(jnp.shape(mean_square), is_left), lax.rsqrt(mean_square), jnp.sqrt(2.0 * bond_right.astype(jnp.float32))
    )
    return (rows * factor)[None]


def local(sites, start, gates, bonds):
    chain_index = lax.axis_index("chain")
    is_left = chain_index % 2 == 0
    left_site = jnp.where(is_left, chain_index, chain_index - 1)
    bond_left = bonds[left_site]
    bond_mid = bonds[left_site + 1]
    bond_right = bonds[left_site + 2]
    bounds = jnp.stack([bond_right, bond_mid, jnp.where(is_left, 0, 1)]).astype(jnp.int32)
    if lax.axis_size("bond") == 4:
        thetas, x, gram = pair_step(gates, bonds, sites[0], start[0])
        inverse = factor_inverse(bounds, gram)
        rows, squares = final_rows(thetas, x, inverse)
        return scaled(rows, total_of(squares), bond_left, bond_mid, bond_right, is_left)
    return spread_out(sites, start, gates, bonds, bounds, is_left, left_site)


def spread_out(sites, start, gates, bonds, bounds, is_left, left_site):
    bond_index = lax.axis_index("bond")
    rank_width = start.shape[2]
    local_rows = sites.shape[1]
    own_site = sites[0]
    own_start = start[0]
    bond_left = bonds[left_site]
    bond_mid = bonds[left_site + 1]
    bond_right = bonds[left_site + 2]
    columns = jnp.arange(rank_width)
    row_global = bond_index * local_rows + jnp.arange(local_rows)
    mid_keep = columns < bond_mid
    other_rows = partner(own_site, "chain", 0)
    a_rows = jnp.where(is_left, own_site, other_rows)
    b_rows = jnp.where(is_left, other_rows, own_site)
    b_full = lax.all_gather(b_rows, "bond", axis=0, tiled=True)
    whole_start = lax.all_gather(own_start, "bond", axis=0, tiled=True)
    other_start = partner(whole_start, "chain", 0)
    starts = jnp.stack(
        [jnp.where(is_left, whole_start, other_start), jnp.where(is_left, other_start, whole_start)]
    )
    left_keep = (row_global < bond_left)[:, None] & jnp.tile(mid_keep, 2)[None, :]
    left_used = jnp.where(left_keep, a_rows, jnp.zeros((), jnp.bfloat16))
    thetas, own = theta_terms(gates[left_site], bounds, left_used, b_full, starts)
    kept_half = jnp.where(is_left, 0, 1)
    half_rows = own.shape[0] // 2
    kept = lax.dynamic_slice_in_dim(own, kept_half * half_rows, half_rows, 0)
    given = lax.dynamic_slice_in_dim(own, (1 - kept_half) * half_rows, half_rows, 0)
    both = (kept.astype(jnp.float32) + partner(given, "chain", 0).astype(jnp.float32)).astype(jnp.bfloat16)
    summed = lax.psum_scatter(both, "bond", scatter_dimension=0, tiled=True)
    own_half = lax.all_gather(summed, "bond", axis=0, tiled=True)
    other_half = partner(own_half, "chain", 0)
    projected_all = jnp.concatenate(
        [jnp.where(is_left, own_half, other_half), jnp.where(is_left, other_half, own_half)], axis=0
    )
    gram = lax.dot_general(
        projected_all, projected_all, (((0,), (0,)), ((), ())), preferred_element_type=jnp.float32
    )
    inverse = factor_inverse(bounds, gram)

    def left_rows():
        reduced = jnp.dot(
            thetas.reshape(2 * local_rows, -1), projected_all, preferred_element_type=jnp.float32
        )
        upper = lax.dot_general(
            reduced,
            inverse,
            (((1,), (1,)), ((), ())),
            precision=lax.Precision.HIGH,
            preferred_element_type=jnp.float32,
        )
        joined = jnp.concatenate([upper[:local_rows], upper[local_rows:]], axis=1)
        return joined, jnp.sum(joined * joined)

    def right_rows():
        block = lax.dynamic_slice_in_dim(inverse, bond_index * local_rows, local_rows, 0)
        basis_rows = lax.dot_general(
            block,
            projected_all.astype(jnp.float32),
            (((1,), (1,)), ((), ())),
            precision=lax.Precision.HIGH,
            preferred_element_type=jnp.float32,
        )
        return basis_rows, jnp.float32(0.0)

    rows, squares = lax.cond(is_left, left_rows, right_rows)
    return scaled(rows, lax.psum(squares, "bond"), bond_left, bond_mid, bond_right, is_left)


def solution(mesh):
    placed = (P("chain", "bond", None), P("chain", "bond", None), P(), P())
    return jax.shard_map(
        local, mesh=mesh, in_specs=placed, out_specs=P("chain", "bond", None), check_vma=False
    )
```

```python
import jax
import jax.numpy as jnp
from jax import lax
from jax.experimental import pallas as pl
from jax.experimental.pallas import tpu as pltpu
from jax.sharding import PartitionSpec as P

ridge_ratio = 0.05
BLOCK = 128
SUB = 8


def partner(value, axis, apart):
    return lax.ppermute(value, axis, [(i, i ^ 1 << apart) for i in range(lax.axis_size(axis))])


def halves(x):
    high = x.astype(jnp.bfloat16)
    return high, (x - high.astype(jnp.float32)).astype(jnp.bfloat16)


def lane_of(x, j):
    return jnp.broadcast_to(x[:, j : j + 1], (SUB, BLOCK))


def row_of(x, j):
    return jnp.broadcast_to(x[j : j + 1, :], (SUB, BLOCK))


def eliminate(rows, first):
    lane = lax.broadcasted_iota(jnp.int32, (SUB, BLOCK), 1)
    sub = lax.broadcasted_iota(jnp.int32, (SUB, BLOCK), 0)
    rows = list(rows)
    for t in range(0, len(rows), 2):
        base = first + t * SUB
        inside = (lane >= base) & (lane < base + 2 * SUB)
        columns = (
            [lane_of(rows[t], base + j) for j in range(SUB)],
            [lane_of(rows[t + 1], base + j) for j in range(2 * SUB)],
        )
        below = range(t + 2, len(rows))
        held = {i: [lane_of(rows[i], base + j) for j in range(2 * SUB)] for i in below}
        current = [
            jnp.where(inside, jnp.where(lane == base + sub + h * SUB, 1.0, 0.0), rows[t + h]) for h in range(2)
        ]
        fresh = {i: jnp.where(inside, 0.0, rows[i]) for i in below}
        pivots = [jnp.ones((SUB, BLOCK), jnp.float32)] * 2
        for j in range(0, 2 * SUB, 2):
            half, local = j // SUB, j % SUB
            source = columns[half]
            a, b, c = row_of(source[j], local), row_of(source[j], local + 1), row_of(source[j + 1], local + 1)
            inverses = [1.0 / a, a * (1.0 / (a * c - b * b))]
            values = [a, c - b * b * inverses[0]]
            for q in (j, j + 1):
                inv, at = inverses[q - j], q % SUB
                pivots[half] = jnp.where(sub == at, values[q - j], pivots[half])
                uppers = {k: row_of(columns[k // SUB][q], k % SUB) for k in range(q + 1, 2 * SUB)}
                row = row_of(current[half], at)
                for h in range(half, 2):
                    m = columns[h][q] * inv
                    for k in range(q + 1, (h + 1) * SUB):
                        columns[h][k] = columns[h][k] - m * uppers[k]
                    current[h] = current[h] - (jnp.where(sub > at, m, 0.0) if h == half else m) * row
                for i in below:
                    m = held[i][q] * inv
                    for k in range(q + 1, 2 * SUB):
                        held[i][k] = held[i][k] - m * uppers[k]
                    fresh[i] = fresh[i] - m * row
        for h in range(2):
            rows[t + h] = current[h] * lax.rsqrt(pivots[h])
        for i in below:
            rows[i] = fresh[i]
    return rows


def threefold(x):
    high, low = halves(x)
    return jnp.concatenate([high, low, high], axis=0)


def threewide(x):
    high, low = halves(x)
    return jnp.concatenate([high, high, low], axis=1)


GROUP = 64


def diagonal_inverse(tile):
    part = GROUP // SUB
    rows = [tile[i * SUB : (i + 1) * SUB, :] for i in range(BLOCK // SUB)]
    for g in range(0, len(rows), part):
        rows[g : g + part] = eliminate(rows[g : g + part], g * SUB)
        if g + part < len(rows):
            done = jnp.concatenate(rows[g : g + part], axis=0)
            line = lax.broadcasted_iota(jnp.int32, done.shape, 0) + g * SUB
            lane = lax.broadcasted_iota(jnp.int32, done.shape, 1)
            right = jnp.where((lane > line) & (lane < (g + part) * SUB), 0.0, done)
            left = done.T[(g + part) * SUB :, :]
            update = jnp.dot(threewide(left), threefold(right), preferred_element_type=jnp.float32)
            lane = lax.broadcasted_iota(jnp.int32, (SUB, BLOCK), 1)
            inside = (lane >= g * SUB) & (lane < (g + part) * SUB)
            for i in range(g + part, len(rows)):
                there = slice((i - g - part) * SUB, (i - g - part + 1) * SUB)
                rows[i] = jnp.where(inside, 0.0, rows[i]) - update[there, :]
    whole = jnp.concatenate(rows, axis=0)
    line = lax.broadcasted_iota(jnp.int32, whole.shape, 0)
    lane = lax.broadcasted_iota(jnp.int32, whole.shape, 1)
    return jnp.where(lane <= line, whole, 0.0)


def turned(x):
    return x.astype(jnp.float32).T.astype(x.dtype)


def factor_kernel(bounds_ref, gram_ref, out_ref, tile_ref, inverse_ref):
    size = out_ref.shape[0]
    count = size // BLOCK
    out_ref[...] = gram_ref[...]
    across = lax.broadcasted_iota(jnp.int32, (BLOCK, BLOCK), 1)
    eye = lax.broadcasted_iota(jnp.int32, (BLOCK, BLOCK), 0) == across
    kept = bounds_ref[1]
    diagonal = jnp.zeros((BLOCK, BLOCK), jnp.float32)
    for i in range(count):
        here = slice(i * BLOCK, (i + 1) * BLOCK)
        diagonal = diagonal + jnp.where(eye, out_ref[here, here], 0.0)
    trace = jnp.sum(jnp.sum(diagonal, axis=0, keepdims=True), axis=1, keepdims=True)
    ridge = ridge_ratio * trace / jnp.full((1, 1), kept, jnp.int32).astype(jnp.float32)
    unit = 1.0 / ridge
    root = lax.rsqrt(ridge)
    for i in range(count):
        here = slice(i * BLOCK, (i + 1) * BLOCK)
        out_ref[here, here] = out_ref[here, here] + jnp.where(eye, ridge, 0.0)
    tile_ref[...] = out_ref[0:BLOCK, 0:BLOCK] * unit
    inverse_ref[...] = jnp.zeros_like(inverse_ref)

    def finish(k, live):
        here = pl.ds(pl.multiple_of(k * BLOCK, BLOCK), BLOCK)
        inverse = inverse_ref[...]
        done = jnp.dot(threewide(inverse), threefold(out_ref[here, :]), preferred_element_type=jnp.float32)
        column = lax.broadcasted_iota(jnp.int32, (BLOCK, size), 1)
        own = (column >= k * BLOCK) & (column < (k + 1) * BLOCK)
        done = jnp.where(own, jnp.concatenate([inverse] * count, axis=1), done)
        out_ref[here, :] = jnp.where(live, jnp.where(column < (k + 1) * BLOCK, done, 0.0), out_ref[here, :])
        return done, own

    def panel(k, carry):
        before = jnp.maximum(k - 1, 0)
        inverse = diagonal_inverse(tile_ref[...]) * root
        done, own = finish(before, k > 0)
        right = threefold(done)
        for i in range(1, count):
            there = slice(i * BLOCK, (i + 1) * BLOCK)
            left = threewide(done[:, there].T)
            left = jnp.where(i >= k, left, jnp.zeros((), left.dtype))
            left = jnp.where(k > 0, left, jnp.zeros((), left.dtype))
            kept_rows = jnp.where((i >= k) & (k > 0) & own, 0.0, out_ref[there, :])
            out_ref[there, :] = kept_rows - jnp.dot(left, right, preferred_element_type=jnp.float32)
        inverse_ref[...] = inverse
        here = pl.ds(pl.multiple_of(k * BLOCK, BLOCK), BLOCK)
        after = pl.ds(pl.multiple_of(jnp.minimum(k + 1, count - 1) * BLOCK, BLOCK), BLOCK)
        across_next = jnp.dot(threewide(inverse), threefold(out_ref[here, after]), preferred_element_type=jnp.float32)
        tile_ref[...] = unit * (
            out_ref[after, after]
            - jnp.dot(threewide(across_next.T), threefold(across_next), preferred_element_type=jnp.float32)
        )
        return carry

    lax.fori_loop(0, count, panel, 0)
    finish(count - 1, kept > 0)


def factor_inverse(bounds, gram):
    size = gram.shape[1]
    return pl.pallas_call(
        factor_kernel,
        out_shape=jax.ShapeDtypeStruct((size, size), jnp.float32),
        in_specs=[pl.BlockSpec(memory_space=pltpu.SMEM), pl.BlockSpec(memory_space=pltpu.VMEM)],
        out_specs=pl.BlockSpec(memory_space=pltpu.VMEM),
        scratch_shapes=[pltpu.VMEM((BLOCK, BLOCK), jnp.float32)] * 2,
    )(bounds, gram)


CHUNK = 256


def theta_kernel(gate_ref, bounds_ref, a_ref, b_ref, start_ref, theta_ref, own_ref, image_ref):
    width = start_ref.shape[1]
    height = a_ref.shape[0]
    kept_right, kept_mid, first = bounds_ref[0], bounds_ref[1], bounds_ref[2]
    lane = lax.broadcasted_iota(jnp.int32, (height, CHUNK), 1)

    def mix(c, carry):
        offset = c * CHUNK
        inside = lane + offset < kept_right
        mixed = []
        for i in range(2):
            for j in range(2):
                columns = pl.ds(pl.multiple_of(j * width + offset, CHUNK), CHUNK)
                product = jnp.dot(
                    a_ref[:, i * width : (i + 1) * width],
                    b_ref[:, columns],
                    preferred_element_type=jnp.float32,
                )
                mixed.append(jnp.where(inside, product, 0.0))
        for o in range(2):
            for q in range(2):
                row = 4 * (2 * o + q)
                value = (
                    gate_ref[row] * mixed[0]
                    + gate_ref[row + 1] * mixed[1]
                    + gate_ref[row + 2] * mixed[2]
                    + gate_ref[row + 3] * mixed[3]
                )
                columns = pl.ds(pl.multiple_of(q * width + offset, CHUNK), CHUNK)
                theta_ref[o, :, columns] = value.astype(jnp.bfloat16)
        return carry

    lax.fori_loop(0, width // CHUNK, mix, 0)

    def image(c, carry):
        columns = pl.ds(pl.multiple_of(c * CHUNK, CHUNK), CHUNK)
        total = jnp.dot(
            theta_ref[first, :, :width], start_ref[0, :, columns], preferred_element_type=jnp.float32
        ) + jnp.dot(
            theta_ref[first, :, width:], start_ref[1, :, columns], preferred_element_type=jnp.float32
        )
        image_ref[:, columns] = jnp.where(lane + c * CHUNK < kept_mid, total, 0.0).astype(jnp.bfloat16)
        return carry

    lax.fori_loop(0, width // CHUNK, image, 0)

    def term(c, carry):
        columns = pl.ds(pl.multiple_of(c * CHUNK, CHUNK), CHUNK)
        own_ref[columns, :] = jnp.dot(
            turned(theta_ref[first, :, columns]), image_ref[...], preferred_element_type=jnp.float32
        ).astype(jnp.bfloat16)
        return carry

    lax.fori_loop(0, 2 * width // CHUNK, term, 0)


def theta_terms(gate, bounds, a_used, b_full, starts):
    height, wide = a_used.shape
    width = starts.shape[2]
    return pl.pallas_call(
        theta_kernel,
        out_shape=(
            jax.ShapeDtypeStruct((2, height, wide), jnp.bfloat16),
            jax.ShapeDtypeStruct((wide, width), jnp.bfloat16),
        ),
        in_specs=[pl.BlockSpec(memory_space=pltpu.SMEM)] * 2 + [pl.BlockSpec(memory_space=pltpu.VMEM)] * 3,
        out_specs=(pl.BlockSpec(memory_space=pltpu.VMEM),) * 2,
        scratch_shapes=[pltpu.VMEM((height, width), jnp.bfloat16)],
    )(gate, bounds, a_used, b_full, starts)


MESH = pl.DeviceIdType.MESH


class Links:
    def __init__(self, send_sem, recv_sem):
        self.chain, self.me = lax.axis_index("chain"), lax.axis_index("bond")
        self.core = self.chain % 2
        self.near = self.me + 1 - 2 * (self.me % 2)
        self.far = (self.me + 2) % 4
        self.across = 3 - self.me
        self.x, self.y, self.d = (self.chain, self.near), (self.chain, self.far), (self.chain, self.across)
        self.mate = (self.chain + 1 - 2 * self.core, self.me)
        self.send_sem, self.recv_sem, self.copies = send_sem, recv_sem, []

    def greet(self, others):
        barrier = pltpu.get_barrier_semaphore()
        for other in others:
            pl.semaphore_signal(barrier, inc=1, device_id=other, device_id_type=MESH)
        pl.semaphore_wait(barrier, len(others))

    def plan(self, source, target, device):
        slot = len(self.copies)
        copy = pltpu.make_async_remote_copy(
            src_ref=source,
            dst_ref=target,
            send_sem=self.send_sem.at[slot],
            recv_sem=self.recv_sem.at[slot],
            device_id=device,
            device_id_type=MESH,
        )
        self.copies.append(copy)
        return copy

    def send(self, source, target, device):
        copy = self.plan(source, target, device)
        copy.start()
        return copy

    def drain(self):
        for copy in self.copies:
            copy.wait_send()


def add(x, y):
    return x.astype(jnp.float32) + y.astype(jnp.float32)


def pair_kernel(
    gate_ref, bond_ref, site_ref, start_ref, out_ref, factor_ref,
    ab, used, b_all, s_all, mixed, image, image_t, own, inc, acc, one, two, theta_ref, x_ref,
    grams, solved, turned_ref, schur, tile_ref, inverses, sides, product_ref, below, whole, reduced, scalars,
    send_sem, recv_sem, local_sem,
):
    links = Links(send_sem, recv_sem)
    links.greet((links.x, links.y, links.d, links.mate))
    core, me, near, far, across = links.core, links.me, links.near, links.far, links.across
    send = links.send
    height, wide = site_ref.shape
    width = wide // 2
    left_site = links.chain - core
    kept_left, kept_mid, kept_right = bond_ref[left_site], bond_ref[left_site + 1], bond_ref[left_site + 2]
    half = height // 2
    quarter = half // 2

    parts = 2
    span = width // parts
    held = pltpu.make_async_copy(site_ref, ab.at[core], local_sem.at[0])
    held.start()
    first = send(site_ref.at[pl.ds(0, half)], ab.at[core, pl.ds(0, half)], links.mate)
    second = send(site_ref.at[pl.ds(half, half)], ab.at[core, pl.ds(half, half)], links.mate)

    def s_block(k, i):
        return s_all.at[k, core, i]

    def s_piece(k, i, p):
        return s_all.at[k, core, i, pl.ds(p * half, half)]

    def s_own(k, p):
        return start_ref.at[pl.ds(p * half, half), pl.ds(k * span, span)]

    starts = []
    for k in range(parts):
        whole_own = start_ref.at[:, pl.ds(k * span, span)]
        starts.append(
            dict(
                held=pltpu.make_async_copy(whole_own, s_block(k, me), local_sem.at[1 + k]),
                mate=links.plan(whole_own, s_block(k, me), links.mate),
                x0=links.plan(s_own(k, 0), s_piece(k, me, 0), links.x),
                y1=links.plan(s_own(k, 1), s_piece(k, me, 1), links.y),
                x1=links.plan(s_own(k, 1), s_piece(k, me, 1), links.x),
                y0=links.plan(s_own(k, 0), s_piece(k, me, 0), links.y),
                forward_y=links.plan(s_piece(k, near, 0), s_piece(k, near, 0), links.y),
                forward_x=links.plan(s_piece(k, far, 1), s_piece(k, far, 1), links.x),
                mate_near=links.plan(s_block(k, near), s_block(k, near), links.mate),
                mate_far=links.plan(s_block(k, far), s_block(k, far), links.mate),
                mate_across=links.plan(s_block(k, across), s_block(k, across), links.mate),
            )
        )

    def s_go(k, *names):
        for name in names:
            starts[k][name].start()

    def s_wait(k, *names):
        for name in names:
            starts[k][name].wait_recv()

    def s_forward(k):
        s_wait(k, "x0")
        s_go(k, "forward_y")
        s_wait(k, "y1")
        s_go(k, "forward_x")

    def s_to_mate(k):
        s_wait(k, "x1")
        s_go(k, "mate_near")
        s_wait(k, "y0")
        s_go(k, "mate_far")
        s_wait(k, "forward_y", "forward_x")
        s_go(k, "mate_across")

    def b_piece(i, p):
        return b_all.at[i, core, pl.ds(p * quarter, quarter)]

    def b_own(p):
        return ab.at[1, pl.ds(pl.multiple_of(core * half + p * quarter, quarter), quarter)]

    s_go(0, "x0", "y1", "mate", "held")
    held.wait()
    first.wait_recv()
    b0x = send(b_own(0), b_piece(me, 0), links.x)
    b1y = send(b_own(1), b_piece(me, 1), links.y)
    second.wait_recv()
    b1x = send(b_own(1), b_piece(me, 1), links.x)
    b0y = send(b_own(0), b_piece(me, 0), links.y)

    line = lax.broadcasted_iota(jnp.int32, (height, CHUNK), 0) + me * height
    lane = lax.broadcasted_iota(jnp.int32, (height, CHUNK), 1)

    def mask(c, carry):
        for i in range(2):
            columns = pl.ds(pl.multiple_of(i * width + c * CHUNK, CHUNK), CHUNK)
            keep = (line < kept_left) & (lane + c * CHUNK < kept_mid)
            used[:, columns] = jnp.where(keep, ab[0, :, columns].astype(jnp.float32), 0.0).astype(jnp.bfloat16)
        return carry

    lax.fori_loop(0, width // CHUNK, mask, 0)
    whole[...] = jnp.zeros_like(whole)

    def mix(load, index, fresh):
        def step(c, carry):
            columns = pl.ds(pl.multiple_of(c * CHUNK, CHUNK), CHUNK)
            right = load(columns)
            for i in range(2):
                left = used[:, pl.ds(pl.multiple_of(i * width + index * height, height), height)]
                product = jnp.dot(left, right, preferred_element_type=jnp.float32)
                mixed[i, :, columns] = product if fresh else mixed[i, :, columns] + product
            return carry

        lax.fori_loop(0, wide // CHUNK, step, 0)

    def gathered(i):
        return lambda columns: b_all[i, :, :, columns].reshape(height, CHUNK)

    mix(lambda columns: ab[1, :, columns], me, True)

    s_forward(0)
    b0x.wait_recv()
    bf_y = send(b_piece(near, 0), b_piece(near, 0), links.y)
    relay_b = [send(b_piece(near, 0), b_piece(near, 0), links.mate)]
    b1y.wait_recv()
    bf_x = send(b_piece(far, 1), b_piece(far, 1), links.x)
    relay_b.append(send(b_piece(far, 1), b_piece(far, 1), links.mate))
    s_go(0, "x1", "y0")
    b1x.wait_recv()
    relay_b.append(send(b_piece(near, 1), b_piece(near, 1), links.mate))
    b0y.wait_recv()
    relay_b.append(send(b_piece(far, 0), b_piece(far, 0), links.mate))
    s_go(1, "x0", "y1", "mate", "held")
    for copy in relay_b:
        copy.wait_recv()
    mix(gathered(near), near, False)
    mix(gathered(far), far, False)
    bf_y.wait_recv()
    last_b = [send(b_piece(across, 0), b_piece(across, 0), links.mate)]
    bf_x.wait_recv()
    last_b.append(send(b_piece(across, 1), b_piece(across, 1), links.mate))
    for copy in last_b:
        copy.wait_recv()
    mix(gathered(across), across, False)

    def form(c, carry):
        offset = c * CHUNK
        inside = lane + offset < kept_right
        parts = []
        for i in range(2):
            for j in range(2):
                columns = pl.ds(pl.multiple_of(j * width + offset, CHUNK), CHUNK)
                parts.append(jnp.where(inside, mixed[i, :, columns], 0.0))
        for o in range(2):
            for q in range(2):
                row = 4 * (2 * o + q)
                value = (
                    gate_ref[left_site, row] * parts[0]
                    + gate_ref[left_site, row + 1] * parts[1]
                    + gate_ref[left_site, row + 2] * parts[2]
                    + gate_ref[left_site, row + 3] * parts[3]
                )
                columns = pl.ds(pl.multiple_of(q * width + offset, CHUNK), CHUNK)
                theta_ref[o, :, columns] = value.astype(jnp.bfloat16)
        return carry

    lax.fori_loop(0, width // CHUNK, form, 0)

    def apply(k, q, i, fresh=False):
        def step(c, carry):
            columns = pl.ds(pl.multiple_of(c * CHUNK, CHUNK), CHUNK)
            there = pl.ds(pl.multiple_of(k * span + c * CHUNK, CHUNK), CHUNK)
            rows = pl.ds(pl.multiple_of(q * width + i * height, height), height)
            product = jnp.dot(
                theta_ref[core, :, rows], s_all[k, q, i, :, columns], preferred_element_type=jnp.float32
            )
            image[:, there] = product if fresh else image[:, there] + product
            return carry

        lax.fori_loop(0, span // CHUNK, step, 0)

    def imaged(k):
        starts[k]["held"].wait()
        apply(k, core, me, True)
        for i in (near, far, across):
            apply(k, core, i)
        s_wait(k, "mate")
        apply(k, 1 - core, me)
        for i, name in ((near, "mate_near"), (far, "mate_far"), (across, "mate_across")):
            s_wait(k, name)
            apply(k, 1 - core, i)

        def turn(c, carry):
            columns = pl.ds(pl.multiple_of(k * span + c * CHUNK, CHUNK), CHUNK)
            kept = lane + k * span + c * CHUNK < kept_mid
            image_t[columns, :] = jnp.where(kept, image[:, columns], 0.0).T.astype(jnp.bfloat16)
            return carry

        lax.fori_loop(0, span // CHUNK, turn, 0)

    def term(k, h, i):
        columns = pl.ds(pl.multiple_of(h * width + i * height, height), height)

        def step(c, carry):
            rows = pl.ds(pl.multiple_of(k * span + c * CHUNK, CHUNK), CHUNK)
            own[h, i, rows, :] = jnp.dot(
                image_t[rows, :], theta_ref[core, :, columns], preferred_element_type=jnp.float32
            ).astype(jnp.bfloat16)
            return carry

        lax.fori_loop(0, span // CHUNK, step, 0)

    order = (across, near, far, me)
    sums = [{} for _ in range(parts)]

    def low(k):
        return pl.ds(k * span, span // 2)

    def high(k):
        return pl.ds(k * span + span // 2, span // 2)

    def exchange(k):
        both = pl.ds(k * span, span)
        sums[k]["swaps"] = []
        for i in order:
            term(k, 1 - core, i)
            sums[k]["swaps"].append(send(own.at[1 - core, i, both], inc.at[i, both], links.mate))

    def reduce_first(k):
        both = pl.ds(k * span, span)

        def merge(position):
            i = order[position]
            term(k, core, i)
            sums[k]["swaps"][position].wait_recv()
            acc[i, both] = add(own[core, i, both], inc[i, both]).astype(jnp.bfloat16)

        merge(0)
        sums[k]["x1"] = send(acc.at[across, low(k)], one.at[k, 0, 1], links.x)
        sums[k]["y1"] = send(acc.at[across, high(k)], one.at[k, 1, 1], links.y)
        merge(1)
        sums[k]["x0"] = send(acc.at[near, low(k)], one.at[k, 0, 0], links.x)
        merge(2)
        sums[k]["y0"] = send(acc.at[far, high(k)], one.at[k, 1, 0], links.y)
        merge(3)

    def reduce_second(k):
        sums[k]["x1"].wait_recv()
        two[k, 2] = add(acc[far, low(k)], one[k, 0, 1]).astype(jnp.bfloat16)
        sums[k]["y2"] = send(two.at[k, 2], two.at[k, 0], links.y)
        sums[k]["y1"].wait_recv()
        two[k, 3] = add(acc[near, high(k)], one[k, 1, 1]).astype(jnp.bfloat16)
        sums[k]["x2"] = send(two.at[k, 3], two.at[k, 1], links.x)

    def reduce_last(k, part):
        for name, n, where in (("0", 0, low(k)), ("1", 1, high(k))):
            sums[k][("x0", "y0")[n]].wait_recv()
            sums[k][("y2", "x2")[n]].wait_recv()
            value = add(acc[me, where], one[k, n, 0]) + two[k, n].astype(jnp.float32)
            value = value.astype(jnp.bfloat16)
            x_ref[core, me, where] = value
            value = value.astype(jnp.float32)
            value = jnp.sum((value * value).reshape(span // 2 // SUB, SUB, height), axis=0)
            for j in range(height // BLOCK):
                part = part + value[:, j * BLOCK : (j + 1) * BLOCK]
        return part

    s_to_mate(0)
    imaged(0)
    s_forward(1)
    s_go(1, "x1", "y0")
    exchange(0)
    reduce_first(0)
    s_to_mate(1)
    reduce_second(0)
    imaged(1)
    exchange(1)
    reduce_first(1)
    part = reduce_last(0, jnp.zeros((SUB, BLOCK), jnp.float32))
    reduce_second(1)

    def piece(i, c, p):
        return x_ref.at[core, i, pl.ds(c * CHUNK + p * BLOCK, BLOCK)]

    def chunk_of(i, c):
        return x_ref.at[core, i, pl.ds(c * CHUNK, CHUNK)]

    chunks = width // CHUNK
    plans = []
    for c in range(chunks):
        plans.append(
            dict(
                y0=links.plan(piece(me, c, 0), piece(me, c, 0), links.y),
                x1=links.plan(piece(me, c, 1), piece(me, c, 1), links.x),
                x0=links.plan(piece(me, c, 0), piece(me, c, 0), links.x),
                y1=links.plan(piece(me, c, 1), piece(me, c, 1), links.y),
                mate=links.plan(chunk_of(me, c), chunk_of(me, c), links.mate),
                forward_x=links.plan(piece(far, c, 0), piece(far, c, 0), links.x),
                forward_y=links.plan(piece(near, c, 1), piece(near, c, 1), links.y),
                mate_near=links.plan(chunk_of(near, c), chunk_of(near, c), links.mate),
                mate_far=links.plan(chunk_of(far, c), chunk_of(far, c), links.mate),
                mate_across=links.plan(chunk_of(across, c), chunk_of(across, c), links.mate),
            )
        )

    def offer(c):
        for name in ("y0", "x1", "x0", "y1", "mate"):
            plans[c][name].start()

    def pass_on(c):
        plans[c]["y0"].wait_recv()
        plans[c]["forward_x"].start()
        plans[c]["x1"].wait_recv()
        plans[c]["forward_y"].start()

    def to_mate(c):
        plans[c]["x0"].wait_recv()
        plans[c]["mate_near"].start()
        plans[c]["y1"].wait_recv()
        plans[c]["mate_far"].start()

    def last_to_mate(c):
        plans[c]["forward_x"].wait_recv()
        plans[c]["forward_y"].wait_recv()
        plans[c]["mate_across"].start()

    def arrive(c):
        for name in ("mate", "mate_near", "mate_far", "mate_across"):
            plans[c][name].wait_recv()

    offer(0)
    part = reduce_last(1, part)

    def spread_sum(value, at, others):
        scalars[at] = value
        copies = [send(scalars.at[at], scalars.at[at + 1 + n], other) for n, other in enumerate(others)]
        for n, copy in enumerate(copies):
            copy.wait_recv()
            value = value + scalars[at + 1 + n]
        return value

    part = spread_sum(part, 0, (links.mate,))
    pass_on(0)
    offer(1)
    part = spread_sum(part, 2, (links.x, links.y, links.d))
    trace = jnp.sum(jnp.sum(part, axis=0, keepdims=True), axis=1, keepdims=True)
    ridge = ridge_ratio * trace / jnp.full((1, 1), kept_mid, jnp.int32).astype(jnp.float32)
    unit, root = 1.0 / ridge, lax.rsqrt(ridge)
    to_mate(0)
    last_to_mate(0)
    arrive(0)

    nt = (((1,), (1,)), ((), ()))
    blocks = [(h, i) for h in range(2) for i in range(width // height)]
    eye = lax.broadcasted_iota(jnp.int32, (CHUNK, CHUNK), 0) == lax.broadcasted_iota(jnp.int32, (CHUNK, CHUNK), 1)
    scalars[6] = jnp.zeros((SUB, BLOCK), jnp.float32)
    inverses[...] = jnp.zeros_like(inverses)
    sides[...] = jnp.zeros_like(sides)

    def upper(c, o, lines):
        reach = (c + 1) * CHUNK
        here = slice(reach - CHUNK, reach)
        value = lax.dot_general(
            jnp.concatenate([reduced[0, lines, :reach], reduced[0, lines, :reach], reduced[1, lines, :reach]], axis=1),
            jnp.concatenate([whole[0, here, :reach], whole[1, here, :reach], whole[0, here, :reach]], axis=1),
            nt, preferred_element_type=jnp.float32,
        )
        out_ref[:, pl.ds(pl.multiple_of(o * width + reach - CHUNK, CHUNK), CHUNK)] = value
        squared = jnp.sum((value * value).reshape(height // SUB, SUB, CHUNK), axis=0)
        part = squared[:, :BLOCK]
        for j in range(1, CHUNK // BLOCK):
            part = part + squared[:, j * BLOCK : (j + 1) * BLOCK]
        scalars[6] = scalars[6] + part

    for c in range(chunks):
        start = c * CHUNK
        reach = start + CHUNK
        here = slice(start, reach)
        for j in range(c + 1):
            value = jnp.zeros((CHUNK, CHUNK), jnp.float32)
            for h, i in blocks:
                value = value + lax.dot_general(
                    x_ref[h, i, j * CHUNK : (j + 1) * CHUNK, :], x_ref[h, i, here, :], nt,
                    preferred_element_type=jnp.float32,
                )
            grams[j * CHUNK : (j + 1) * CHUNK, :] = value
        value = grams[here, :]
        if c > 0:
            for j in range(c):
                to = (j + 1) * CHUNK
                row = slice(j * CHUNK, to)
                solved[row, :] = jnp.dot(
                    jnp.concatenate([whole[0, row, :to], whole[0, row, :to], whole[1, row, :to]], axis=1),
                    threefold(grams[:to, :]),
                    preferred_element_type=jnp.float32,
                )
            turned_ref[:, : 3 * start] = threewide(solved[:start, :].T)
            value = value - jnp.dot(
                turned_ref[:, : 3 * start], threefold(solved[:start, :]), preferred_element_type=jnp.float32
            )
        schur[...] = value + jnp.where(eye, ridge, 0.0)
        tile_ref[...] = unit * schur[:BLOCK, :BLOCK]

        def panel(p, carry, c=c, start=start):
            lines = pl.ds(pl.multiple_of(p * BLOCK, BLOCK), BLOCK)
            columns = pl.ds(pl.multiple_of(start + p * BLOCK, BLOCK), BLOCK)
            inverse = diagonal_inverse(tile_ref[...]) * root
            value = jnp.zeros((2 * height, BLOCK), jnp.float32)
            for h, i in blocks:
                at = h * width + i * height
                value = value + lax.dot_general(
                    theta_ref[:, :, at : at + height].reshape(2 * height, height), x_ref[h, i, columns, :], nt,
                    preferred_element_type=jnp.float32,
                )
            top, low_part = halves(value)
            reduced[0, :, columns] = top
            reduced[1, :, columns] = low_part
            if c > 0:
                product_ref[lines, :start] = jnp.dot(
                    turned_ref[lines, : 3 * start],
                    jnp.concatenate([whole[0, :start, :start], whole[1, :start, :start], whole[0, :start, :start]], axis=0),
                    preferred_element_type=jnp.float32,
                )
            if c > 0:
                upper(c - 1, p, pl.ds(pl.multiple_of(p * height, height), height))
            below[...] = jnp.dot(threewide(sides[...].T), threefold(inverses[0]), preferred_element_type=jnp.float32)
            inverses[p] = inverse

            @pl.when(p == 0)
            def _():
                side = jnp.dot(threewide(inverses[0]), threefold(schur[:BLOCK, BLOCK:]), preferred_element_type=jnp.float32)
                sides[...] = side
                tile_ref[...] = unit * (
                    schur[BLOCK:, BLOCK:]
                    - jnp.dot(threewide(side.T), threefold(side), preferred_element_type=jnp.float32)
                )
                if c + 1 < chunks:
                    pass_on(c + 1)
                    to_mate(c + 1)
                    if c + 2 < chunks:
                        offer(c + 2)

            if c + 1 < chunks:

                @pl.when(p == 1)
                def _():
                    last_to_mate(c + 1)

            return carry

        lax.fori_loop(0, CHUNK // BLOCK, panel, 0)
        corner = -jnp.dot(threewide(inverses[1]), threefold(below[...]), preferred_element_type=jnp.float32)
        own_inverse = jnp.concatenate(
            [
                jnp.concatenate([inverses[0], jnp.zeros((BLOCK, BLOCK), jnp.float32)], axis=1),
                jnp.concatenate([corner, inverses[1]], axis=1),
            ],
            axis=0,
        )
        top, low_part = halves(own_inverse)
        whole[0, here, here] = top
        whole[1, here, here] = low_part
        if c > 0:
            lead = -jnp.dot(
                jnp.concatenate([top, top, low_part], axis=1), threefold(product_ref[:, :start]),
                preferred_element_type=jnp.float32,
            )
            top, low_part = halves(lead)
            whole[0, here, :start] = top
            whole[1, here, :start] = low_part

        if c + 1 < chunks:
            arrive(c + 1)

    @pl.when(core == 0)
    def _():
        for o in range(2):
            upper(chunks - 1, o, slice(o * height, (o + 1) * height))

    @pl.when(core == 1)
    def _():
        rows = pl.ds(pl.multiple_of(me * height, height), height)
        for h, i in blocks:
            at = h * width + i * height
            out_ref[:, at : at + height] = jnp.dot(
                whole[0, rows, :], x_ref[h, i], preferred_element_type=jnp.float32
            ) + jnp.dot(whole[1, rows, :], x_ref[h, i], preferred_element_type=jnp.float32)

    total = spread_sum(scalars[6], 7, (links.x, links.y, links.d))
    total = jnp.sum(jnp.sum(total, axis=0, keepdims=True), axis=1, keepdims=True)

    def real(value):
        return jnp.full((1, 1), value, jnp.int32).astype(jnp.float32)

    mean_square = total / (2.0 * real(kept_left) * real(kept_mid)) + 1e-06
    factor = jnp.where(core == 0, lax.rsqrt(mean_square), jnp.sqrt(2.0 * real(kept_right)))
    factor_ref[...] = jnp.broadcast_to(factor, (SUB, BLOCK))
    links.drain()


def pair_step(gates, bonds, own_site, own_start):
    rows, wide = own_site.shape
    width = wide // 2
    n = lax.axis_size("bond")
    kind = jnp.bfloat16
    copies = 112
    return pl.pallas_call(
        pair_kernel,
        out_shape=(
            jax.ShapeDtypeStruct((rows, wide), jnp.float32),
            jax.ShapeDtypeStruct((SUB, BLOCK), jnp.float32),
        ),
        in_specs=[pl.BlockSpec(memory_space=pltpu.SMEM)] * 2 + [pl.BlockSpec(memory_space=pltpu.HBM)] * 2,
        out_specs=(pl.BlockSpec(memory_space=pltpu.VMEM),) * 2,
        scratch_shapes=[
            pltpu.VMEM((2, rows, wide), kind),
            pltpu.VMEM((rows, wide), kind),
            pltpu.VMEM((n, 2, rows // 2, wide), kind),
            pltpu.VMEM((2, 2, n, rows, width // 2), kind),
            pltpu.VMEM((2, rows, wide), jnp.float32),
            pltpu.VMEM((rows, width), jnp.float32),
            pltpu.VMEM((width, rows), kind),
            pltpu.VMEM((2, n, width, rows), kind),
            pltpu.VMEM((n, width, rows), kind),
            pltpu.VMEM((n, width, rows), kind),
            pltpu.VMEM((2, 2, 2, width // 4, rows), kind),
            pltpu.VMEM((2, 4, width // 4, rows), kind),
            pltpu.VMEM((2, rows, wide), kind),
            pltpu.VMEM((2, n, width, rows), kind),
            pltpu.VMEM((width, CHUNK), jnp.float32),
            pltpu.VMEM((width, CHUNK), jnp.float32),
            pltpu.VMEM((CHUNK, 3 * width), kind),
            pltpu.VMEM((CHUNK, CHUNK), jnp.float32),
            pltpu.VMEM((BLOCK, BLOCK), jnp.float32),
            pltpu.VMEM((2, BLOCK, BLOCK), jnp.float32),
            pltpu.VMEM((BLOCK, BLOCK), jnp.float32),
            pltpu.VMEM((CHUNK, width), jnp.float32),
            pltpu.VMEM((BLOCK, BLOCK), jnp.float32),
            pltpu.VMEM((2, width, width), kind),
            pltpu.VMEM((2, 2 * rows, width), kind),
            pltpu.VMEM((11, SUB, BLOCK), jnp.float32),
            pltpu.SemaphoreType.DMA((copies,)),
            pltpu.SemaphoreType.DMA((copies,)),
            pltpu.SemaphoreType.DMA((3,)),
        ],
        compiler_params=pltpu.CompilerParams(
            collective_id=0, has_side_effects=True, vmem_limit_bytes=57 * 1024 * 1024
        ),
    )(gates, bonds, own_site, own_start)


def scaled(rows, sum_squares, bond_left, bond_mid, bond_right, is_left):
    mean_square = (
        sum_squares / (2.0 * bond_left.astype(jnp.float32) * bond_mid.astype(jnp.float32)) + 1e-06
    )
    factor = jnp.where(
        jnp.full(jnp.shape(mean_square), is_left), lax.rsqrt(mean_square), jnp.sqrt(2.0 * bond_right.astype(jnp.float32))
    )
    return (rows * factor)[None]


def local(sites, start, gates, bonds):
    if lax.axis_size("bond") == 4:
        rows, factor = pair_step(gates, bonds, sites[0], start[0])
        return (rows * factor[:1, :1])[None]
    return spread_out(sites, start, gates, bonds)


def spread_out(sites, start, gates, bonds):
    bond_index = lax.axis_index("bond")
    chain_index = lax.axis_index("chain")
    is_left = chain_index % 2 == 0
    left_site = jnp.where(is_left, chain_index, chain_index - 1)
    rank_width = start.shape[2]
    local_rows = sites.shape[1]
    own_site = sites[0]
    own_start = start[0]
    bond_left = bonds[left_site]
    bond_mid = bonds[left_site + 1]
    bond_right = bonds[left_site + 2]
    bounds = jnp.stack([bond_right, bond_mid, jnp.where(is_left, 0, 1)]).astype(jnp.int32)
    columns = jnp.arange(rank_width)
    row_global = bond_index * local_rows + jnp.arange(local_rows)
    mid_keep = columns < bond_mid
    other_rows = partner(own_site, "chain", 0)
    a_rows = jnp.where(is_left, own_site, other_rows)
    b_rows = jnp.where(is_left, other_rows, own_site)
    b_full = lax.all_gather(b_rows, "bond", axis=0, tiled=True)
    whole_start = lax.all_gather(own_start, "bond", axis=0, tiled=True)
    other_start = partner(whole_start, "chain", 0)
    starts = jnp.stack(
        [jnp.where(is_left, whole_start, other_start), jnp.where(is_left, other_start, whole_start)]
    )
    left_keep = (row_global < bond_left)[:, None] & jnp.tile(mid_keep, 2)[None, :]
    left_used = jnp.where(left_keep, a_rows, jnp.zeros((), jnp.bfloat16))
    thetas, own = theta_terms(gates[left_site], bounds, left_used, b_full, starts)
    kept_half = jnp.where(is_left, 0, 1)
    half_rows = own.shape[0] // 2
    kept = lax.dynamic_slice_in_dim(own, kept_half * half_rows, half_rows, 0)
    given = lax.dynamic_slice_in_dim(own, (1 - kept_half) * half_rows, half_rows, 0)
    both = (kept.astype(jnp.float32) + partner(given, "chain", 0).astype(jnp.float32)).astype(jnp.bfloat16)
    summed = lax.psum_scatter(both, "bond", scatter_dimension=0, tiled=True)
    own_half = lax.all_gather(summed, "bond", axis=0, tiled=True)
    other_half = partner(own_half, "chain", 0)
    projected_all = jnp.concatenate(
        [jnp.where(is_left, own_half, other_half), jnp.where(is_left, other_half, own_half)], axis=0
    )
    gram = lax.dot_general(
        projected_all, projected_all, (((0,), (0,)), ((), ())), preferred_element_type=jnp.float32
    )
    inverse = factor_inverse(bounds, gram)

    def left_rows():
        reduced = jnp.dot(
            thetas.reshape(2 * local_rows, -1), projected_all, preferred_element_type=jnp.float32
        )
        upper = lax.dot_general(
            reduced,
            inverse,
            (((1,), (1,)), ((), ())),
            precision=lax.Precision.HIGH,
            preferred_element_type=jnp.float32,
        )
        joined = jnp.concatenate([upper[:local_rows], upper[local_rows:]], axis=1)
        return joined, jnp.sum(joined * joined)

    def right_rows():
        block = lax.dynamic_slice_in_dim(inverse, bond_index * local_rows, local_rows, 0)
        basis_rows = lax.dot_general(
            block,
            projected_all.astype(jnp.float32),
            (((1,), (1,)), ((), ())),
            precision=lax.Precision.HIGH,
            preferred_element_type=jnp.float32,
        )
        return basis_rows, jnp.float32(0.0)

    rows, squares = lax.cond(is_left, left_rows, right_rows)
    return scaled(rows, lax.psum(squares, "bond"), bond_left, bond_mid, bond_right, is_left)


def solution(mesh):
    placed = (P("chain", "bond", None), P("chain", "bond", None), P(), P())
    return jax.shard_map(
        local, mesh=mesh, in_specs=placed, out_specs=P("chain", "bond", None), check_vma=False
    )
```

```python
import jax
import jax.numpy as jnp
from jax import lax
from jax.experimental import pallas as pl
from jax.experimental.pallas import tpu as pltpu
from jax.sharding import PartitionSpec as P

ridge_ratio = 0.05
BLOCK = 128
SUB = 8


def partner(value, axis, apart):
    return lax.ppermute(value, axis, [(i, i ^ 1 << apart) for i in range(lax.axis_size(axis))])


def halves(x):
    high = x.astype(jnp.bfloat16)
    return high, (x - high.astype(jnp.float32)).astype(jnp.bfloat16)


def lane_of(x, j):
    return jnp.broadcast_to(x[:, j : j + 1], (SUB, BLOCK))


def row_of(x, j):
    return jnp.broadcast_to(x[j : j + 1, :], (SUB, BLOCK))


def eliminate(rows, first):
    lane = lax.broadcasted_iota(jnp.int32, (SUB, BLOCK), 1)
    sub = lax.broadcasted_iota(jnp.int32, (SUB, BLOCK), 0)
    rows = list(rows)
    for t in range(0, len(rows), 2):
        base = first + t * SUB
        inside = (lane >= base) & (lane < base + 2 * SUB)
        columns = (
            [lane_of(rows[t], base + j) for j in range(SUB)],
            [lane_of(rows[t + 1], base + j) for j in range(2 * SUB)],
        )
        below = range(t + 2, len(rows))
        held = {i: [lane_of(rows[i], base + j) for j in range(2 * SUB)] for i in below}
        current = [
            jnp.where(inside, jnp.where(lane == base + sub + h * SUB, 1.0, 0.0), rows[t + h]) for h in range(2)
        ]
        fresh = {i: jnp.where(inside, 0.0, rows[i]) for i in below}
        pivots = [jnp.ones((SUB, BLOCK), jnp.float32)] * 2
        for j in range(0, 2 * SUB, 2):
            half, local = j // SUB, j % SUB
            source = columns[half]
            a, b, c = row_of(source[j], local), row_of(source[j], local + 1), row_of(source[j + 1], local + 1)
            inverses = [1.0 / a, a * (1.0 / (a * c - b * b))]
            values = [a, c - b * b * inverses[0]]
            for q in (j, j + 1):
                inv, at = inverses[q - j], q % SUB
                pivots[half] = jnp.where(sub == at, values[q - j], pivots[half])
                uppers = {k: row_of(columns[k // SUB][q], k % SUB) for k in range(q + 1, 2 * SUB)}
                row = row_of(current[half], at)
                for h in range(half, 2):
                    m = columns[h][q] * inv
                    for k in range(q + 1, (h + 1) * SUB):
                        columns[h][k] = columns[h][k] - m * uppers[k]
                    current[h] = current[h] - (jnp.where(sub > at, m, 0.0) if h == half else m) * row
                for i in below:
                    m = held[i][q] * inv
                    for k in range(q + 1, 2 * SUB):
                        held[i][k] = held[i][k] - m * uppers[k]
                    fresh[i] = fresh[i] - m * row
        for h in range(2):
            rows[t + h] = current[h] * lax.rsqrt(pivots[h])
        for i in below:
            rows[i] = fresh[i]
    return rows


def threefold(x):
    high, low = halves(x)
    return jnp.concatenate([high, low, high], axis=0)


def threewide(x):
    high, low = halves(x)
    return jnp.concatenate([high, high, low], axis=1)


GROUP = 64


def diagonal_inverse(tile):
    part = GROUP // SUB
    rows = [tile[i * SUB : (i + 1) * SUB, :] for i in range(BLOCK // SUB)]
    for g in range(0, len(rows), part):
        rows[g : g + part] = eliminate(rows[g : g + part], g * SUB)
        if g + part < len(rows):
            done = jnp.concatenate(rows[g : g + part], axis=0)
            line = lax.broadcasted_iota(jnp.int32, done.shape, 0) + g * SUB
            lane = lax.broadcasted_iota(jnp.int32, done.shape, 1)
            right = jnp.where((lane > line) & (lane < (g + part) * SUB), 0.0, done)
            left = done.T[(g + part) * SUB :, :]
            update = jnp.dot(threewide(left), threefold(right), preferred_element_type=jnp.float32)
            lane = lax.broadcasted_iota(jnp.int32, (SUB, BLOCK), 1)
            inside = (lane >= g * SUB) & (lane < (g + part) * SUB)
            for i in range(g + part, len(rows)):
                there = slice((i - g - part) * SUB, (i - g - part + 1) * SUB)
                rows[i] = jnp.where(inside, 0.0, rows[i]) - update[there, :]
    whole = jnp.concatenate(rows, axis=0)
    line = lax.broadcasted_iota(jnp.int32, whole.shape, 0)
    lane = lax.broadcasted_iota(jnp.int32, whole.shape, 1)
    return jnp.where(lane <= line, whole, 0.0)


def turned(x):
    return x.astype(jnp.float32).T.astype(x.dtype)


def factor_kernel(bounds_ref, gram_ref, out_ref, tile_ref, inverse_ref):
    size = out_ref.shape[0]
    count = size // BLOCK
    out_ref[...] = gram_ref[...]
    across = lax.broadcasted_iota(jnp.int32, (BLOCK, BLOCK), 1)
    eye = lax.broadcasted_iota(jnp.int32, (BLOCK, BLOCK), 0) == across
    kept = bounds_ref[1]
    diagonal = jnp.zeros((BLOCK, BLOCK), jnp.float32)
    for i in range(count):
        here = slice(i * BLOCK, (i + 1) * BLOCK)
        diagonal = diagonal + jnp.where(eye, out_ref[here, here], 0.0)
    trace = jnp.sum(jnp.sum(diagonal, axis=0, keepdims=True), axis=1, keepdims=True)
    ridge = ridge_ratio * trace / jnp.full((1, 1), kept, jnp.int32).astype(jnp.float32)
    unit = 1.0 / ridge
    root = lax.rsqrt(ridge)
    for i in range(count):
        here = slice(i * BLOCK, (i + 1) * BLOCK)
        out_ref[here, here] = out_ref[here, here] + jnp.where(eye, ridge, 0.0)
    tile_ref[...] = out_ref[0:BLOCK, 0:BLOCK] * unit
    inverse_ref[...] = jnp.zeros_like(inverse_ref)

    def finish(k, live):
        here = pl.ds(pl.multiple_of(k * BLOCK, BLOCK), BLOCK)
        inverse = inverse_ref[...]
        done = jnp.dot(threewide(inverse), threefold(out_ref[here, :]), preferred_element_type=jnp.float32)
        column = lax.broadcasted_iota(jnp.int32, (BLOCK, size), 1)
        own = (column >= k * BLOCK) & (column < (k + 1) * BLOCK)
        done = jnp.where(own, jnp.concatenate([inverse] * count, axis=1), done)
        out_ref[here, :] = jnp.where(live, jnp.where(column < (k + 1) * BLOCK, done, 0.0), out_ref[here, :])
        return done, own

    def panel(k, carry):
        before = jnp.maximum(k - 1, 0)
        inverse = diagonal_inverse(tile_ref[...]) * root
        done, own = finish(before, k > 0)
        right = threefold(done)
        for i in range(1, count):
            there = slice(i * BLOCK, (i + 1) * BLOCK)
            left = threewide(done[:, there].T)
            left = jnp.where(i >= k, left, jnp.zeros((), left.dtype))
            left = jnp.where(k > 0, left, jnp.zeros((), left.dtype))
            kept_rows = jnp.where((i >= k) & (k > 0) & own, 0.0, out_ref[there, :])
            out_ref[there, :] = kept_rows - jnp.dot(left, right, preferred_element_type=jnp.float32)
        inverse_ref[...] = inverse
        here = pl.ds(pl.multiple_of(k * BLOCK, BLOCK), BLOCK)
        after = pl.ds(pl.multiple_of(jnp.minimum(k + 1, count - 1) * BLOCK, BLOCK), BLOCK)
        across_next = jnp.dot(threewide(inverse), threefold(out_ref[here, after]), preferred_element_type=jnp.float32)
        tile_ref[...] = unit * (
            out_ref[after, after]
            - jnp.dot(threewide(across_next.T), threefold(across_next), preferred_element_type=jnp.float32)
        )
        return carry

    lax.fori_loop(0, count, panel, 0)
    finish(count - 1, kept > 0)


def factor_inverse(bounds, gram):
    size = gram.shape[1]
    return pl.pallas_call(
        factor_kernel,
        out_shape=jax.ShapeDtypeStruct((size, size), jnp.float32),
        in_specs=[pl.BlockSpec(memory_space=pltpu.SMEM), pl.BlockSpec(memory_space=pltpu.VMEM)],
        out_specs=pl.BlockSpec(memory_space=pltpu.VMEM),
        scratch_shapes=[pltpu.VMEM((BLOCK, BLOCK), jnp.float32)] * 2,
    )(bounds, gram)


CHUNK = 256


def theta_kernel(gate_ref, bounds_ref, a_ref, b_ref, start_ref, theta_ref, own_ref, image_ref):
    width = start_ref.shape[1]
    height = a_ref.shape[0]
    kept_right, kept_mid, first = bounds_ref[0], bounds_ref[1], bounds_ref[2]
    lane = lax.broadcasted_iota(jnp.int32, (height, CHUNK), 1)

    def mix(c, carry):
        offset = c * CHUNK
        inside = lane + offset < kept_right
        mixed = []
        for i in range(2):
            for j in range(2):
                columns = pl.ds(pl.multiple_of(j * width + offset, CHUNK), CHUNK)
                product = jnp.dot(
                    a_ref[:, i * width : (i + 1) * width],
                    b_ref[:, columns],
                    preferred_element_type=jnp.float32,
                )
                mixed.append(jnp.where(inside, product, 0.0))
        for o in range(2):
            for q in range(2):
                row = 4 * (2 * o + q)
                value = (
                    gate_ref[row] * mixed[0]
                    + gate_ref[row + 1] * mixed[1]
                    + gate_ref[row + 2] * mixed[2]
                    + gate_ref[row + 3] * mixed[3]
                )
                columns = pl.ds(pl.multiple_of(q * width + offset, CHUNK), CHUNK)
                theta_ref[o, :, columns] = value.astype(jnp.bfloat16)
        return carry

    lax.fori_loop(0, width // CHUNK, mix, 0)

    def image(c, carry):
        columns = pl.ds(pl.multiple_of(c * CHUNK, CHUNK), CHUNK)
        total = jnp.dot(
            theta_ref[first, :, :width], start_ref[0, :, columns], preferred_element_type=jnp.float32
        ) + jnp.dot(
            theta_ref[first, :, width:], start_ref[1, :, columns], preferred_element_type=jnp.float32
        )
        image_ref[:, columns] = jnp.where(lane + c * CHUNK < kept_mid, total, 0.0).astype(jnp.bfloat16)
        return carry

    lax.fori_loop(0, width // CHUNK, image, 0)

    def term(c, carry):
        columns = pl.ds(pl.multiple_of(c * CHUNK, CHUNK), CHUNK)
        own_ref[columns, :] = jnp.dot(
            turned(theta_ref[first, :, columns]), image_ref[...], preferred_element_type=jnp.float32
        ).astype(jnp.bfloat16)
        return carry

    lax.fori_loop(0, 2 * width // CHUNK, term, 0)


def theta_terms(gate, bounds, a_used, b_full, starts):
    height, wide = a_used.shape
    width = starts.shape[2]
    return pl.pallas_call(
        theta_kernel,
        out_shape=(
            jax.ShapeDtypeStruct((2, height, wide), jnp.bfloat16),
            jax.ShapeDtypeStruct((wide, width), jnp.bfloat16),
        ),
        in_specs=[pl.BlockSpec(memory_space=pltpu.SMEM)] * 2 + [pl.BlockSpec(memory_space=pltpu.VMEM)] * 3,
        out_specs=(pl.BlockSpec(memory_space=pltpu.VMEM),) * 2,
        scratch_shapes=[pltpu.VMEM((height, width), jnp.bfloat16)],
    )(gate, bounds, a_used, b_full, starts)


MESH = pl.DeviceIdType.MESH


class Links:
    def __init__(self, send_sem, recv_sem):
        self.chain, self.me = lax.axis_index("chain"), lax.axis_index("bond")
        self.core = self.chain % 2
        self.near = self.me + 1 - 2 * (self.me % 2)
        self.far = (self.me + 2) % 4
        self.across = 3 - self.me
        self.x, self.y, self.d = (self.chain, self.near), (self.chain, self.far), (self.chain, self.across)
        self.mate = (self.chain + 1 - 2 * self.core, self.me)
        self.send_sem, self.recv_sem, self.copies = send_sem, recv_sem, []

    def greet(self, others):
        barrier = pltpu.get_barrier_semaphore()
        for other in others:
            pl.semaphore_signal(barrier, inc=1, device_id=other, device_id_type=MESH)
        pl.semaphore_wait(barrier, len(others))

    def plan(self, source, target, device):
        slot = len(self.copies)
        copy = pltpu.make_async_remote_copy(
            src_ref=source,
            dst_ref=target,
            send_sem=self.send_sem.at[slot],
            recv_sem=self.recv_sem.at[slot],
            device_id=device,
            device_id_type=MESH,
        )
        self.copies.append(copy)
        return copy

    def send(self, source, target, device):
        copy = self.plan(source, target, device)
        copy.start()
        return copy

    def drain(self):
        for copy in self.copies:
            copy.wait_send()


def add(x, y):
    return x.astype(jnp.float32) + y.astype(jnp.float32)


def pair_kernel(
    gate_ref, bond_ref, site_ref, start_ref, out_ref, factor_ref,
    ab, used, b_all, s_all, mixed, image, image_t, own, inc, acc, one, two, theta_ref, x_ref,
    grams, solved, turned_ref, schur, tile_ref, inverses, sides, product_ref, below, whole, reduced, scalars,
    send_sem, recv_sem, local_sem,
):
    links = Links(send_sem, recv_sem)
    links.greet((links.x, links.y, links.d, links.mate))
    core, me, near, far, across = links.core, links.me, links.near, links.far, links.across
    send = links.send
    height, wide = site_ref.shape
    width = wide // 2
    left_site = links.chain - core
    kept_left, kept_mid, kept_right = bond_ref[left_site], bond_ref[left_site + 1], bond_ref[left_site + 2]
    half = height // 2
    quarter = half // 2

    parts = 2
    span = width // parts
    held = pltpu.make_async_copy(site_ref, ab.at[core], local_sem.at[0])
    held.start()
    first = send(site_ref.at[pl.ds(0, half)], ab.at[core, pl.ds(0, half)], links.mate)
    second = send(site_ref.at[pl.ds(half, half)], ab.at[core, pl.ds(half, half)], links.mate)

    def s_block(k, i):
        return s_all.at[k, core, i]

    def s_piece(k, i, p):
        return s_all.at[k, core, i, pl.ds(p * half, half)]

    def s_own(k, p):
        return start_ref.at[pl.ds(p * half, half), pl.ds(k * span, span)]

    starts = []
    for k in range(parts):
        whole_own = start_ref.at[:, pl.ds(k * span, span)]
        starts.append(
            dict(
                held=pltpu.make_async_copy(whole_own, s_block(k, me), local_sem.at[1 + k]),
                mate=links.plan(whole_own, s_block(k, me), links.mate),
                x0=links.plan(s_own(k, 0), s_piece(k, me, 0), links.x),
                y1=links.plan(s_own(k, 1), s_piece(k, me, 1), links.y),
                x1=links.plan(s_own(k, 1), s_piece(k, me, 1), links.x),
                y0=links.plan(s_own(k, 0), s_piece(k, me, 0), links.y),
                forward_y=links.plan(s_piece(k, near, 0), s_piece(k, near, 0), links.y),
                forward_x=links.plan(s_piece(k, far, 1), s_piece(k, far, 1), links.x),
                mate_near=links.plan(s_block(k, near), s_block(k, near), links.mate),
                mate_far=links.plan(s_block(k, far), s_block(k, far), links.mate),
                mate_across=links.plan(s_block(k, across), s_block(k, across), links.mate),
            )
        )

    def s_go(k, *names):
        for name in names:
            starts[k][name].start()

    def s_wait(k, *names):
        for name in names:
            starts[k][name].wait_recv()

    def s_forward(k):
        s_wait(k, "x0")
        s_go(k, "forward_y")
        s_wait(k, "y1")
        s_go(k, "forward_x")

    def s_to_mate(k):
        s_wait(k, "x1")
        s_go(k, "mate_near")
        s_wait(k, "y0")
        s_go(k, "mate_far")
        s_wait(k, "forward_y", "forward_x")
        s_go(k, "mate_across")

    def b_piece(i, p):
        return b_all.at[i, core, pl.ds(p * quarter, quarter)]

    def b_own(p):
        return ab.at[1, pl.ds(pl.multiple_of(core * half + p * quarter, quarter), quarter)]

    s_go(0, "x0", "y1", "mate", "held")
    held.wait()
    first.wait_recv()
    b0x = send(b_own(0), b_piece(me, 0), links.x)
    b1y = send(b_own(1), b_piece(me, 1), links.y)
    second.wait_recv()
    b1x = send(b_own(1), b_piece(me, 1), links.x)
    b0y = send(b_own(0), b_piece(me, 0), links.y)

    line = lax.broadcasted_iota(jnp.int32, (height, CHUNK), 0) + me * height
    lane = lax.broadcasted_iota(jnp.int32, (height, CHUNK), 1)

    def mask(c, carry):
        for i in range(2):
            columns = pl.ds(pl.multiple_of(i * width + c * CHUNK, CHUNK), CHUNK)
            keep = (line < kept_left) & (lane + c * CHUNK < kept_mid)
            used[:, columns] = jnp.where(keep, ab[0, :, columns].astype(jnp.float32), 0.0).astype(jnp.bfloat16)
        return carry

    lax.fori_loop(0, width // CHUNK, mask, 0)
    whole[...] = jnp.zeros_like(whole)

    def mix(load, index, fresh):
        def step(c, carry):
            columns = pl.ds(pl.multiple_of(c * CHUNK, CHUNK), CHUNK)
            right = load(columns)
            for i in range(2):
                left = used[:, pl.ds(pl.multiple_of(i * width + index * height, height), height)]
                product = jnp.dot(left, right, preferred_element_type=jnp.float32)
                mixed[i, :, columns] = product if fresh else mixed[i, :, columns] + product
            return carry

        lax.fori_loop(0, wide // CHUNK, step, 0)

    def gathered(i):
        return lambda columns: b_all[i, :, :, columns].reshape(height, CHUNK)

    mix(lambda columns: ab[1, :, columns], me, True)

    s_forward(0)
    b0x.wait_recv()
    bf_y = send(b_piece(near, 0), b_piece(near, 0), links.y)
    relay_b = [send(b_piece(near, 0), b_piece(near, 0), links.mate)]
    b1y.wait_recv()
    bf_x = send(b_piece(far, 1), b_piece(far, 1), links.x)
    relay_b.append(send(b_piece(far, 1), b_piece(far, 1), links.mate))
    s_go(0, "x1", "y0")
    b1x.wait_recv()
    relay_b.append(send(b_piece(near, 1), b_piece(near, 1), links.mate))
    b0y.wait_recv()
    relay_b.append(send(b_piece(far, 0), b_piece(far, 0), links.mate))
    s_go(1, "x0", "y1", "mate", "held")
    for copy in relay_b:
        copy.wait_recv()
    mix(gathered(near), near, False)
    mix(gathered(far), far, False)
    bf_y.wait_recv()
    last_b = [send(b_piece(across, 0), b_piece(across, 0), links.mate)]
    bf_x.wait_recv()
    last_b.append(send(b_piece(across, 1), b_piece(across, 1), links.mate))
    for copy in last_b:
        copy.wait_recv()
    mix(gathered(across), across, False)

    def form(c, carry):
        offset = c * CHUNK
        inside = lane + offset < kept_right
        parts = []
        for i in range(2):
            for j in range(2):
                columns = pl.ds(pl.multiple_of(j * width + offset, CHUNK), CHUNK)
                parts.append(jnp.where(inside, mixed[i, :, columns], 0.0))
        for o in range(2):
            for q in range(2):
                row = 4 * (2 * o + q)
                value = (
                    gate_ref[left_site, row] * parts[0]
                    + gate_ref[left_site, row + 1] * parts[1]
                    + gate_ref[left_site, row + 2] * parts[2]
                    + gate_ref[left_site, row + 3] * parts[3]
                )
                columns = pl.ds(pl.multiple_of(q * width + offset, CHUNK), CHUNK)
                theta_ref[o, :, columns] = value.astype(jnp.bfloat16)
        return carry

    lax.fori_loop(0, width // CHUNK, form, 0)

    def apply(k, q, i, fresh=False):
        def step(c, carry):
            columns = pl.ds(pl.multiple_of(c * CHUNK, CHUNK), CHUNK)
            there = pl.ds(pl.multiple_of(k * span + c * CHUNK, CHUNK), CHUNK)
            rows = pl.ds(pl.multiple_of(q * width + i * height, height), height)
            product = jnp.dot(
                theta_ref[core, :, rows], s_all[k, q, i, :, columns], preferred_element_type=jnp.float32
            )
            image[:, there] = product if fresh else image[:, there] + product
            return carry

        lax.fori_loop(0, span // CHUNK, step, 0)

    def imaged(k):
        starts[k]["held"].wait()
        apply(k, core, me, True)
        for i in (near, far, across):
            apply(k, core, i)
        s_wait(k, "mate")
        apply(k, 1 - core, me)
        for i, name in ((near, "mate_near"), (far, "mate_far"), (across, "mate_across")):
            s_wait(k, name)
            apply(k, 1 - core, i)

        def turn(c, carry):
            columns = pl.ds(pl.multiple_of(k * span + c * CHUNK, CHUNK), CHUNK)
            kept = lane + k * span + c * CHUNK < kept_mid
            image_t[columns, :] = jnp.where(kept, image[:, columns], 0.0).T.astype(jnp.bfloat16)
            return carry

        lax.fori_loop(0, span // CHUNK, turn, 0)

    def term(k, h, i):
        columns = pl.ds(pl.multiple_of(h * width + i * height, height), height)

        def step(c, carry):
            rows = pl.ds(pl.multiple_of(k * span + c * CHUNK, CHUNK), CHUNK)
            own[h, i, rows, :] = jnp.dot(
                image_t[rows, :], theta_ref[core, :, columns], preferred_element_type=jnp.float32
            ).astype(jnp.bfloat16)
            return carry

        lax.fori_loop(0, span // CHUNK, step, 0)

    order = (across, near, far, me)
    sums = [{} for _ in range(parts)]

    def low(k):
        return pl.ds(k * span, span // 2)

    def high(k):
        return pl.ds(k * span + span // 2, span // 2)

    def exchange(k):
        both = pl.ds(k * span, span)
        sums[k]["swaps"] = []
        for i in order:
            term(k, 1 - core, i)
            sums[k]["swaps"].append(send(own.at[1 - core, i, both], inc.at[i, both], links.mate))

    def reduce_first(k):
        both = pl.ds(k * span, span)

        def merge(position):
            i = order[position]
            term(k, core, i)
            sums[k]["swaps"][position].wait_recv()
            acc[i, both] = add(own[core, i, both], inc[i, both]).astype(jnp.bfloat16)

        merge(0)
        sums[k]["x1"] = send(acc.at[across, low(k)], one.at[k, 0, 1], links.x)
        sums[k]["y1"] = send(acc.at[across, high(k)], one.at[k, 1, 1], links.y)
        merge(1)
        sums[k]["x0"] = send(acc.at[near, low(k)], one.at[k, 0, 0], links.x)
        merge(2)
        sums[k]["y0"] = send(acc.at[far, high(k)], one.at[k, 1, 0], links.y)
        merge(3)

    def reduce_second(k):
        sums[k]["x1"].wait_recv()
        two[k, 2] = add(acc[far, low(k)], one[k, 0, 1]).astype(jnp.bfloat16)
        sums[k]["y2"] = send(two.at[k, 2], two.at[k, 0], links.y)
        sums[k]["y1"].wait_recv()
        two[k, 3] = add(acc[near, high(k)], one[k, 1, 1]).astype(jnp.bfloat16)
        sums[k]["x2"] = send(two.at[k, 3], two.at[k, 1], links.x)

    def reduce_last(k, part):
        for name, n, where in (("0", 0, low(k)), ("1", 1, high(k))):
            sums[k][("x0", "y0")[n]].wait_recv()
            sums[k][("y2", "x2")[n]].wait_recv()
            value = add(acc[me, where], one[k, n, 0]) + two[k, n].astype(jnp.float32)
            value = value.astype(jnp.bfloat16)
            x_ref[core, me, where] = value
            value = value.astype(jnp.float32)
            value = jnp.sum((value * value).reshape(span // 2 // SUB, SUB, height), axis=0)
            for j in range(height // BLOCK):
                part = part + value[:, j * BLOCK : (j + 1) * BLOCK]
        return part

    s_to_mate(0)
    imaged(0)
    s_forward(1)
    s_go(1, "x1", "y0")
    exchange(0)
    reduce_first(0)
    s_to_mate(1)
    reduce_second(0)
    imaged(1)
    exchange(1)
    reduce_first(1)
    part = reduce_last(0, jnp.zeros((SUB, BLOCK), jnp.float32))
    reduce_second(1)

    def piece(i, c, p):
        return x_ref.at[core, i, pl.ds(c * CHUNK + p * BLOCK, BLOCK)]

    def chunk_of(i, c):
        return x_ref.at[core, i, pl.ds(c * CHUNK, CHUNK)]

    chunks = width // CHUNK
    plans = []
    for c in range(chunks):
        plans.append(
            dict(
                y0=links.plan(piece(me, c, 0), piece(me, c, 0), links.y),
                x1=links.plan(piece(me, c, 1), piece(me, c, 1), links.x),
                x0=links.plan(piece(me, c, 0), piece(me, c, 0), links.x),
                y1=links.plan(piece(me, c, 1), piece(me, c, 1), links.y),
                mate=links.plan(chunk_of(me, c), chunk_of(me, c), links.mate),
                forward_x=links.plan(piece(far, c, 0), piece(far, c, 0), links.x),
                forward_y=links.plan(piece(near, c, 1), piece(near, c, 1), links.y),
                mate_near=links.plan(chunk_of(near, c), chunk_of(near, c), links.mate),
                mate_far=links.plan(chunk_of(far, c), chunk_of(far, c), links.mate),
                mate_across=links.plan(chunk_of(across, c), chunk_of(across, c), links.mate),
            )
        )

    def offer(c):
        for name in ("y0", "x1", "x0", "y1", "mate"):
            plans[c][name].start()

    def pass_on(c):
        plans[c]["y0"].wait_recv()
        plans[c]["forward_x"].start()
        plans[c]["x1"].wait_recv()
        plans[c]["forward_y"].start()

    def to_mate(c):
        plans[c]["x0"].wait_recv()
        plans[c]["mate_near"].start()
        plans[c]["y1"].wait_recv()
        plans[c]["mate_far"].start()

    def last_to_mate(c):
        plans[c]["forward_x"].wait_recv()
        plans[c]["forward_y"].wait_recv()
        plans[c]["mate_across"].start()

    def arrive(c):
        for name in ("mate", "mate_near", "mate_far", "mate_across"):
            plans[c][name].wait_recv()

    offer(0)
    part = reduce_last(1, part)

    def spread_sum(value, at, others):
        scalars[at] = value
        copies = [send(scalars.at[at], scalars.at[at + 1 + n], other) for n, other in enumerate(others)]
        for n, copy in enumerate(copies):
            copy.wait_recv()
            value = value + scalars[at + 1 + n]
        return value

    part = spread_sum(part, 0, (links.mate,))
    pass_on(0)
    offer(1)
    part = spread_sum(part, 2, (links.x, links.y, links.d))
    trace = jnp.sum(jnp.sum(part, axis=0, keepdims=True), axis=1, keepdims=True)
    ridge = ridge_ratio * trace / jnp.full((1, 1), kept_mid, jnp.int32).astype(jnp.float32)
    unit, root = 1.0 / ridge, lax.rsqrt(ridge)
    to_mate(0)
    last_to_mate(0)
    arrive(0)

    nt = (((1,), (1,)), ((), ()))
    blocks = [(h, i) for h in range(2) for i in range(width // height)]
    eye = lax.broadcasted_iota(jnp.int32, (CHUNK, CHUNK), 0) == lax.broadcasted_iota(jnp.int32, (CHUNK, CHUNK), 1)
    scalars[6] = jnp.zeros((SUB, BLOCK), jnp.float32)
    inverses[...] = jnp.zeros_like(inverses)
    sides[...] = jnp.zeros_like(sides)

    def upper(c, o, lines):
        reach = (c + 1) * CHUNK
        here = slice(reach - CHUNK, reach)
        value = lax.dot_general(
            jnp.concatenate([reduced[0, lines, :reach], reduced[0, lines, :reach], reduced[1, lines, :reach]], axis=1),
            jnp.concatenate([whole[0, here, :reach], whole[1, here, :reach], whole[0, here, :reach]], axis=1),
            nt, preferred_element_type=jnp.float32,
        )
        out_ref[:, pl.ds(pl.multiple_of(o * width + reach - CHUNK, CHUNK), CHUNK)] = value
        squared = jnp.sum((value * value).reshape(height // SUB, SUB, CHUNK), axis=0)
        part = squared[:, :BLOCK]
        for j in range(1, CHUNK // BLOCK):
            part = part + squared[:, j * BLOCK : (j + 1) * BLOCK]
        scalars[6] = scalars[6] + part

    for c in range(chunks):
        start = c * CHUNK
        reach = start + CHUNK
        here = slice(start, reach)
        for j in range(c + 1):
            value = jnp.zeros((CHUNK, CHUNK), jnp.float32)
            for h, i in blocks:
                value = value + lax.dot_general(
                    x_ref[h, i, j * CHUNK : (j + 1) * CHUNK, :], x_ref[h, i, here, :], nt,
                    preferred_element_type=jnp.float32,
                )
            grams[j * CHUNK : (j + 1) * CHUNK, :] = value
        value = grams[here, :]
        if c > 0:
            for j in range(c):
                to = (j + 1) * CHUNK
                row = slice(j * CHUNK, to)
                solved[row, :] = jnp.dot(
                    jnp.concatenate([whole[0, row, :to], whole[0, row, :to], whole[1, row, :to]], axis=1),
                    threefold(grams[:to, :]),
                    preferred_element_type=jnp.float32,
                )
            turned_ref[:, : 3 * start] = threewide(solved[:start, :].T)
            value = value - jnp.dot(
                turned_ref[:, : 3 * start], threefold(solved[:start, :]), preferred_element_type=jnp.float32
            )
        schur[...] = value + jnp.where(eye, ridge, 0.0)
        tile_ref[...] = unit * schur[:BLOCK, :BLOCK]

        def panel(p, carry, c=c, start=start):
            lines = pl.ds(pl.multiple_of(p * BLOCK, BLOCK), BLOCK)
            columns = pl.ds(pl.multiple_of(start + p * BLOCK, BLOCK), BLOCK)
            inverse = diagonal_inverse(tile_ref[...]) * root
            value = jnp.zeros((2 * height, BLOCK), jnp.float32)
            for h, i in blocks:
                at = h * width + i * height
                value = value + lax.dot_general(
                    theta_ref[:, :, at : at + height].reshape(2 * height, height), x_ref[h, i, columns, :], nt,
                    preferred_element_type=jnp.float32,
                )
            top, low_part = halves(value)
            reduced[0, :, columns] = top
            reduced[1, :, columns] = low_part
            if c > 0:
                product_ref[lines, :start] = jnp.dot(
                    turned_ref[lines, : 3 * start],
                    jnp.concatenate([whole[0, :start, :start], whole[1, :start, :start], whole[0, :start, :start]], axis=0),
                    preferred_element_type=jnp.float32,
                )
            if c > 0:
                upper(c - 1, p, pl.ds(pl.multiple_of(p * height, height), height))
            below[...] = jnp.dot(threewide(sides[...].T), threefold(inverses[0]), preferred_element_type=jnp.float32)
            inverses[p] = inverse

            @pl.when(p == 0)
            def _():
                side = jnp.dot(threewide(inverses[0]), threefold(schur[:BLOCK, BLOCK:]), preferred_element_type=jnp.float32)
                sides[...] = side
                tile_ref[...] = unit * (
                    schur[BLOCK:, BLOCK:]
                    - jnp.dot(threewide(side.T), threefold(side), preferred_element_type=jnp.float32)
                )
                if c + 1 < chunks:
                    to_mate(c + 1)
                    last_to_mate(c + 1)

            return carry

        if c + 1 < chunks:
            pass_on(c + 1)
        if c + 2 < chunks:
            offer(c + 2)
        lax.fori_loop(0, CHUNK // BLOCK, panel, 0)
        if c + 1 < chunks:
            arrive(c + 1)
        corner = -jnp.dot(threewide(inverses[1]), threefold(below[...]), preferred_element_type=jnp.float32)
        own_inverse = jnp.concatenate(
            [
                jnp.concatenate([inverses[0], jnp.zeros((BLOCK, BLOCK), jnp.float32)], axis=1),
                jnp.concatenate([corner, inverses[1]], axis=1),
            ],
            axis=0,
        )
        top, low_part = halves(own_inverse)
        whole[0, here, here] = top
        whole[1, here, here] = low_part
        if c > 0:
            lead = -jnp.dot(
                jnp.concatenate([top, top, low_part], axis=1), threefold(product_ref[:, :start]),
                preferred_element_type=jnp.float32,
            )
            top, low_part = halves(lead)
            whole[0, here, :start] = top
            whole[1, here, :start] = low_part

    @pl.when(core == 0)
    def _():
        for o in range(2):
            upper(chunks - 1, o, slice(o * height, (o + 1) * height))

    @pl.when(core == 1)
    def _():
        rows = pl.ds(pl.multiple_of(me * height, height), height)
        for h, i in blocks:
            at = h * width + i * height
            out_ref[:, at : at + height] = jnp.dot(
                whole[0, rows, :], x_ref[h, i], preferred_element_type=jnp.float32
            ) + jnp.dot(whole[1, rows, :], x_ref[h, i], preferred_element_type=jnp.float32)

    total = spread_sum(scalars[6], 7, (links.x, links.y, links.d))
    total = jnp.sum(jnp.sum(total, axis=0, keepdims=True), axis=1, keepdims=True)

    def real(value):
        return jnp.full((1, 1), value, jnp.int32).astype(jnp.float32)

    mean_square = total / (2.0 * real(kept_left) * real(kept_mid)) + 1e-06
    factor = jnp.where(core == 0, lax.rsqrt(mean_square), jnp.sqrt(2.0 * real(kept_right)))
    factor_ref[...] = factor
    links.drain()


def pair_step(gates, bonds, own_site, own_start):
    rows, wide = own_site.shape
    width = wide // 2
    n = lax.axis_size("bond")
    kind = jnp.bfloat16
    copies = 112
    return pl.pallas_call(
        pair_kernel,
        out_shape=(
            jax.ShapeDtypeStruct((rows, wide), jnp.float32),
            jax.ShapeDtypeStruct((1, 1), jnp.float32),
        ),
        in_specs=[pl.BlockSpec(memory_space=pltpu.SMEM)] * 2 + [pl.BlockSpec(memory_space=pltpu.HBM)] * 2,
        out_specs=(pl.BlockSpec(memory_space=pltpu.VMEM),) * 2,
        scratch_shapes=[
            pltpu.VMEM((2, rows, wide), kind),
            pltpu.VMEM((rows, wide), kind),
            pltpu.VMEM((n, 2, rows // 2, wide), kind),
            pltpu.VMEM((2, 2, n, rows, width // 2), kind),
            pltpu.VMEM((2, rows, wide), jnp.float32),
            pltpu.VMEM((rows, width), jnp.float32),
            pltpu.VMEM((width, rows), kind),
            pltpu.VMEM((2, n, width, rows), kind),
            pltpu.VMEM((n, width, rows), kind),
            pltpu.VMEM((n, width, rows), kind),
            pltpu.VMEM((2, 2, 2, width // 4, rows), kind),
            pltpu.VMEM((2, 4, width // 4, rows), kind),
            pltpu.VMEM((2, rows, wide), kind),
            pltpu.VMEM((2, n, width, rows), kind),
            pltpu.VMEM((width, CHUNK), jnp.float32),
            pltpu.VMEM((width, CHUNK), jnp.float32),
            pltpu.VMEM((CHUNK, 3 * width), kind),
            pltpu.VMEM((CHUNK, CHUNK), jnp.float32),
            pltpu.VMEM((BLOCK, BLOCK), jnp.float32),
            pltpu.VMEM((2, BLOCK, BLOCK), jnp.float32),
            pltpu.VMEM((BLOCK, BLOCK), jnp.float32),
            pltpu.VMEM((CHUNK, width), jnp.float32),
            pltpu.VMEM((BLOCK, BLOCK), jnp.float32),
            pltpu.VMEM((2, width, width), kind),
            pltpu.VMEM((2, 2 * rows, width), kind),
            pltpu.VMEM((11, SUB, BLOCK), jnp.float32),
            pltpu.SemaphoreType.DMA((copies,)),
            pltpu.SemaphoreType.DMA((copies,)),
            pltpu.SemaphoreType.DMA((3,)),
        ],
        compiler_params=pltpu.CompilerParams(
            collective_id=0, has_side_effects=True, vmem_limit_bytes=57 * 1024 * 1024
        ),
    )(gates, bonds, own_site, own_start)


def scaled(rows, sum_squares, bond_left, bond_mid, bond_right, is_left):
    mean_square = (
        sum_squares / (2.0 * bond_left.astype(jnp.float32) * bond_mid.astype(jnp.float32)) + 1e-06
    )
    factor = jnp.where(
        jnp.full(jnp.shape(mean_square), is_left), lax.rsqrt(mean_square), jnp.sqrt(2.0 * bond_right.astype(jnp.float32))
    )
    return (rows * factor)[None]


def local(sites, start, gates, bonds):
    if lax.axis_size("bond") == 4:
        rows, factor = pair_step(gates, bonds, sites[0], start[0])
        return (rows * factor)[None]
    return spread_out(sites, start, gates, bonds)


def spread_out(sites, start, gates, bonds):
    bond_index = lax.axis_index("bond")
    chain_index = lax.axis_index("chain")
    is_left = chain_index % 2 == 0
    left_site = jnp.where(is_left, chain_index, chain_index - 1)
    rank_width = start.shape[2]
    local_rows = sites.shape[1]
    own_site = sites[0]
    own_start = start[0]
    bond_left = bonds[left_site]
    bond_mid = bonds[left_site + 1]
    bond_right = bonds[left_site + 2]
    bounds = jnp.stack([bond_right, bond_mid, jnp.where(is_left, 0, 1)]).astype(jnp.int32)
    columns = jnp.arange(rank_width)
    row_global = bond_index * local_rows + jnp.arange(local_rows)
    mid_keep = columns < bond_mid
    other_rows = partner(own_site, "chain", 0)
    a_rows = jnp.where(is_left, own_site, other_rows)
    b_rows = jnp.where(is_left, other_rows, own_site)
    b_full = lax.all_gather(b_rows, "bond", axis=0, tiled=True)
    whole_start = lax.all_gather(own_start, "bond", axis=0, tiled=True)
    other_start = partner(whole_start, "chain", 0)
    starts = jnp.stack(
        [jnp.where(is_left, whole_start, other_start), jnp.where(is_left, other_start, whole_start)]
    )
    left_keep = (row_global < bond_left)[:, None] & jnp.tile(mid_keep, 2)[None, :]
    left_used = jnp.where(left_keep, a_rows, jnp.zeros((), jnp.bfloat16))
    thetas, own = theta_terms(gates[left_site], bounds, left_used, b_full, starts)
    kept_half = jnp.where(is_left, 0, 1)
    half_rows = own.shape[0] // 2
    kept = lax.dynamic_slice_in_dim(own, kept_half * half_rows, half_rows, 0)
    given = lax.dynamic_slice_in_dim(own, (1 - kept_half) * half_rows, half_rows, 0)
    both = (kept.astype(jnp.float32) + partner(given, "chain", 0).astype(jnp.float32)).astype(jnp.bfloat16)
    summed = lax.psum_scatter(both, "bond", scatter_dimension=0, tiled=True)
    own_half = lax.all_gather(summed, "bond", axis=0, tiled=True)
    other_half = partner(own_half, "chain", 0)
    projected_all = jnp.concatenate(
        [jnp.where(is_left, own_half, other_half), jnp.where(is_left, other_half, own_half)], axis=0
    )
    gram = lax.dot_general(
        projected_all, projected_all, (((0,), (0,)), ((), ())), preferred_element_type=jnp.float32
    )
    inverse = factor_inverse(bounds, gram)

    def left_rows():
        reduced = jnp.dot(
            thetas.reshape(2 * local_rows, -1), projected_all, preferred_element_type=jnp.float32
        )
        upper = lax.dot_general(
            reduced,
            inverse,
            (((1,), (1,)), ((), ())),
            precision=lax.Precision.HIGH,
            preferred_element_type=jnp.float32,
        )
        joined = jnp.concatenate([upper[:local_rows], upper[local_rows:]], axis=1)
        return joined, jnp.sum(joined * joined)

    def right_rows():
        block = lax.dynamic_slice_in_dim(inverse, bond_index * local_rows, local_rows, 0)
        basis_rows = lax.dot_general(
            block,
            projected_all.astype(jnp.float32),
            (((1,), (1,)), ((), ())),
            precision=lax.Precision.HIGH,
            preferred_element_type=jnp.float32,
        )
        return basis_rows, jnp.float32(0.0)

    rows, squares = lax.cond(is_left, left_rows, right_rows)
    return scaled(rows, lax.psum(squares, "bond"), bond_left, bond_mid, bond_right, is_left)


def solution(mesh):
    placed = (P("chain", "bond", None), P("chain", "bond", None), P(), P())
    return jax.shard_map(
        local, mesh=mesh, in_specs=placed, out_specs=P("chain", "bond", None), check_vma=False
    )
```

```python
import jax
import jax.numpy as jnp
from jax import lax
from jax.experimental import pallas as pl
from jax.experimental.pallas import tpu as pltpu
from jax.sharding import PartitionSpec as P

ridge_ratio = 0.05
BLOCK = 128
SUB = 8


def partner(value, axis, apart):
    return lax.ppermute(value, axis, [(i, i ^ 1 << apart) for i in range(lax.axis_size(axis))])


def halves(x):
    high = x.astype(jnp.bfloat16)
    return high, (x - high.astype(jnp.float32)).astype(jnp.bfloat16)


def lane_of(x, j):
    return jnp.broadcast_to(x[:, j : j + 1], (SUB, BLOCK))


def row_of(x, j):
    return jnp.broadcast_to(x[j : j + 1, :], (SUB, BLOCK))


def eliminate(rows, first):
    lane = lax.broadcasted_iota(jnp.int32, (SUB, BLOCK), 1)
    sub = lax.broadcasted_iota(jnp.int32, (SUB, BLOCK), 0)
    rows = list(rows)
    for t in range(0, len(rows), 2):
        base = first + t * SUB
        inside = (lane >= base) & (lane < base + 2 * SUB)
        columns = (
            [lane_of(rows[t], base + j) for j in range(SUB)],
            [lane_of(rows[t + 1], base + j) for j in range(2 * SUB)],
        )
        below = range(t + 2, len(rows))
        held = {i: [lane_of(rows[i], base + j) for j in range(2 * SUB)] for i in below}
        current = [
            jnp.where(inside, jnp.where(lane == base + sub + h * SUB, 1.0, 0.0), rows[t + h]) for h in range(2)
        ]
        fresh = {i: jnp.where(inside, 0.0, rows[i]) for i in below}
        pivots = [jnp.ones((SUB, BLOCK), jnp.float32)] * 2
        for j in range(0, 2 * SUB, 2):
            half, local = j // SUB, j % SUB
            source = columns[half]
            a, b, c = row_of(source[j], local), row_of(source[j], local + 1), row_of(source[j + 1], local + 1)
            inverses = [1.0 / a, a * (1.0 / (a * c - b * b))]
            values = [a, c - b * b * inverses[0]]
            for q in (j, j + 1):
                inv, at = inverses[q - j], q % SUB
                pivots[half] = jnp.where(sub == at, values[q - j], pivots[half])
                uppers = {k: row_of(columns[k // SUB][q], k % SUB) for k in range(q + 1, 2 * SUB)}
                row = row_of(current[half], at)
                for h in range(half, 2):
                    m = columns[h][q] * inv
                    for k in range(q + 1, (h + 1) * SUB):
                        columns[h][k] = columns[h][k] - m * uppers[k]
                    current[h] = current[h] - (jnp.where(sub > at, m, 0.0) if h == half else m) * row
                for i in below:
                    m = held[i][q] * inv
                    for k in range(q + 1, 2 * SUB):
                        held[i][k] = held[i][k] - m * uppers[k]
                    fresh[i] = fresh[i] - m * row
        for h in range(2):
            rows[t + h] = current[h] * lax.rsqrt(pivots[h])
        for i in below:
            rows[i] = fresh[i]
    return rows


def threefold(x):
    high, low = halves(x)
    return jnp.concatenate([high, low, high], axis=0)


def threewide(x):
    high, low = halves(x)
    return jnp.concatenate([high, high, low], axis=1)


GROUP = 64


def diagonal_inverse(tile):
    part = GROUP // SUB
    rows = [tile[i * SUB : (i + 1) * SUB, :] for i in range(BLOCK // SUB)]
    for g in range(0, len(rows), part):
        rows[g : g + part] = eliminate(rows[g : g + part], g * SUB)
        if g + part < len(rows):
            done = jnp.concatenate(rows[g : g + part], axis=0)
            line = lax.broadcasted_iota(jnp.int32, done.shape, 0) + g * SUB
            lane = lax.broadcasted_iota(jnp.int32, done.shape, 1)
            right = jnp.where((lane > line) & (lane < (g + part) * SUB), 0.0, done)
            left = done.T[(g + part) * SUB :, :]
            update = jnp.dot(threewide(left), threefold(right), preferred_element_type=jnp.float32)
            lane = lax.broadcasted_iota(jnp.int32, (SUB, BLOCK), 1)
            inside = (lane >= g * SUB) & (lane < (g + part) * SUB)
            for i in range(g + part, len(rows)):
                there = slice((i - g - part) * SUB, (i - g - part + 1) * SUB)
                rows[i] = jnp.where(inside, 0.0, rows[i]) - update[there, :]
    whole = jnp.concatenate(rows, axis=0)
    line = lax.broadcasted_iota(jnp.int32, whole.shape, 0)
    lane = lax.broadcasted_iota(jnp.int32, whole.shape, 1)
    return jnp.where(lane <= line, whole, 0.0)


def turned(x):
    return x.astype(jnp.float32).T.astype(x.dtype)


def factor_kernel(bounds_ref, gram_ref, out_ref, tile_ref, inverse_ref):
    size = out_ref.shape[0]
    count = size // BLOCK
    out_ref[...] = gram_ref[...]
    across = lax.broadcasted_iota(jnp.int32, (BLOCK, BLOCK), 1)
    eye = lax.broadcasted_iota(jnp.int32, (BLOCK, BLOCK), 0) == across
    kept = bounds_ref[1]
    diagonal = jnp.zeros((BLOCK, BLOCK), jnp.float32)
    for i in range(count):
        here = slice(i * BLOCK, (i + 1) * BLOCK)
        diagonal = diagonal + jnp.where(eye, out_ref[here, here], 0.0)
    trace = jnp.sum(jnp.sum(diagonal, axis=0, keepdims=True), axis=1, keepdims=True)
    ridge = ridge_ratio * trace / jnp.full((1, 1), kept, jnp.int32).astype(jnp.float32)
    unit = 1.0 / ridge
    root = lax.rsqrt(ridge)
    for i in range(count):
        here = slice(i * BLOCK, (i + 1) * BLOCK)
        out_ref[here, here] = out_ref[here, here] + jnp.where(eye, ridge, 0.0)
    tile_ref[...] = out_ref[0:BLOCK, 0:BLOCK] * unit
    inverse_ref[...] = jnp.zeros_like(inverse_ref)

    def finish(k, live):
        here = pl.ds(pl.multiple_of(k * BLOCK, BLOCK), BLOCK)
        inverse = inverse_ref[...]
        done = jnp.dot(threewide(inverse), threefold(out_ref[here, :]), preferred_element_type=jnp.float32)
        column = lax.broadcasted_iota(jnp.int32, (BLOCK, size), 1)
        own = (column >= k * BLOCK) & (column < (k + 1) * BLOCK)
        done = jnp.where(own, jnp.concatenate([inverse] * count, axis=1), done)
        out_ref[here, :] = jnp.where(live, jnp.where(column < (k + 1) * BLOCK, done, 0.0), out_ref[here, :])
        return done, own

    def panel(k, carry):
        before = jnp.maximum(k - 1, 0)
        inverse = diagonal_inverse(tile_ref[...]) * root
        done, own = finish(before, k > 0)
        right = threefold(done)
        for i in range(1, count):
            there = slice(i * BLOCK, (i + 1) * BLOCK)
            left = threewide(done[:, there].T)
            left = jnp.where(i >= k, left, jnp.zeros((), left.dtype))
            left = jnp.where(k > 0, left, jnp.zeros((), left.dtype))
            kept_rows = jnp.where((i >= k) & (k > 0) & own, 0.0, out_ref[there, :])
            out_ref[there, :] = kept_rows - jnp.dot(left, right, preferred_element_type=jnp.float32)
        inverse_ref[...] = inverse
        here = pl.ds(pl.multiple_of(k * BLOCK, BLOCK), BLOCK)
        after = pl.ds(pl.multiple_of(jnp.minimum(k + 1, count - 1) * BLOCK, BLOCK), BLOCK)
        across_next = jnp.dot(threewide(inverse), threefold(out_ref[here, after]), preferred_element_type=jnp.float32)
        tile_ref[...] = unit * (
            out_ref[after, after]
            - jnp.dot(threewide(across_next.T), threefold(across_next), preferred_element_type=jnp.float32)
        )
        return carry

    lax.fori_loop(0, count, panel, 0)
    finish(count - 1, kept > 0)


def factor_inverse(bounds, gram):
    size = gram.shape[1]
    return pl.pallas_call(
        factor_kernel,
        out_shape=jax.ShapeDtypeStruct((size, size), jnp.float32),
        in_specs=[pl.BlockSpec(memory_space=pltpu.SMEM), pl.BlockSpec(memory_space=pltpu.VMEM)],
        out_specs=pl.BlockSpec(memory_space=pltpu.VMEM),
        scratch_shapes=[pltpu.VMEM((BLOCK, BLOCK), jnp.float32)] * 2,
    )(bounds, gram)


CHUNK = 256


def theta_kernel(gate_ref, bounds_ref, a_ref, b_ref, start_ref, theta_ref, own_ref, image_ref):
    width = start_ref.shape[1]
    height = a_ref.shape[0]
    kept_right, kept_mid, first = bounds_ref[0], bounds_ref[1], bounds_ref[2]
    lane = lax.broadcasted_iota(jnp.int32, (height, CHUNK), 1)

    def mix(c, carry):
        offset = c * CHUNK
        inside = lane + offset < kept_right
        mixed = []
        for i in range(2):
            for j in range(2):
                columns = pl.ds(pl.multiple_of(j * width + offset, CHUNK), CHUNK)
                product = jnp.dot(
                    a_ref[:, i * width : (i + 1) * width],
                    b_ref[:, columns],
                    preferred_element_type=jnp.float32,
                )
                mixed.append(jnp.where(inside, product, 0.0))
        for o in range(2):
            for q in range(2):
                row = 4 * (2 * o + q)
                value = (
                    gate_ref[row] * mixed[0]
                    + gate_ref[row + 1] * mixed[1]
                    + gate_ref[row + 2] * mixed[2]
                    + gate_ref[row + 3] * mixed[3]
                )
                columns = pl.ds(pl.multiple_of(q * width + offset, CHUNK), CHUNK)
                theta_ref[o, :, columns] = value.astype(jnp.bfloat16)
        return carry

    lax.fori_loop(0, width // CHUNK, mix, 0)

    def image(c, carry):
        columns = pl.ds(pl.multiple_of(c * CHUNK, CHUNK), CHUNK)
        total = jnp.dot(
            theta_ref[first, :, :width], start_ref[0, :, columns], preferred_element_type=jnp.float32
        ) + jnp.dot(
            theta_ref[first, :, width:], start_ref[1, :, columns], preferred_element_type=jnp.float32
        )
        image_ref[:, columns] = jnp.where(lane + c * CHUNK < kept_mid, total, 0.0).astype(jnp.bfloat16)
        return carry

    lax.fori_loop(0, width // CHUNK, image, 0)

    def term(c, carry):
        columns = pl.ds(pl.multiple_of(c * CHUNK, CHUNK), CHUNK)
        own_ref[columns, :] = jnp.dot(
            turned(theta_ref[first, :, columns]), image_ref[...], preferred_element_type=jnp.float32
        ).astype(jnp.bfloat16)
        return carry

    lax.fori_loop(0, 2 * width // CHUNK, term, 0)


def theta_terms(gate, bounds, a_used, b_full, starts):
    height, wide = a_used.shape
    width = starts.shape[2]
    return pl.pallas_call(
        theta_kernel,
        out_shape=(
            jax.ShapeDtypeStruct((2, height, wide), jnp.bfloat16),
            jax.ShapeDtypeStruct((wide, width), jnp.bfloat16),
        ),
        in_specs=[pl.BlockSpec(memory_space=pltpu.SMEM)] * 2 + [pl.BlockSpec(memory_space=pltpu.VMEM)] * 3,
        out_specs=(pl.BlockSpec(memory_space=pltpu.VMEM),) * 2,
        scratch_shapes=[pltpu.VMEM((height, width), jnp.bfloat16)],
    )(gate, bounds, a_used, b_full, starts)


MESH = pl.DeviceIdType.MESH


class Links:
    def __init__(self, send_sem, recv_sem):
        self.chain, self.me = lax.axis_index("chain"), lax.axis_index("bond")
        self.core = self.chain % 2
        self.near = self.me + 1 - 2 * (self.me % 2)
        self.far = (self.me + 2) % 4
        self.across = 3 - self.me
        self.x, self.y, self.d = (self.chain, self.near), (self.chain, self.far), (self.chain, self.across)
        self.mate = (self.chain + 1 - 2 * self.core, self.me)
        self.send_sem, self.recv_sem, self.copies = send_sem, recv_sem, []

    def greet(self, others):
        barrier = pltpu.get_barrier_semaphore()
        for other in others:
            pl.semaphore_signal(barrier, inc=1, device_id=other, device_id_type=MESH)
        pl.semaphore_wait(barrier, len(others))

    def plan(self, source, target, device):
        slot = len(self.copies)
        copy = pltpu.make_async_remote_copy(
            src_ref=source,
            dst_ref=target,
            send_sem=self.send_sem.at[slot],
            recv_sem=self.recv_sem.at[slot],
            device_id=device,
            device_id_type=MESH,
        )
        self.copies.append(copy)
        return copy

    def send(self, source, target, device):
        copy = self.plan(source, target, device)
        copy.start()
        return copy

    def drain(self):
        for copy in self.copies:
            copy.wait_send()


def add(x, y):
    return x.astype(jnp.float32) + y.astype(jnp.float32)


def pair_kernel(
    gate_ref, bond_ref, site_ref, start_ref, out_ref, factor_ref,
    ab, used, b_all, s_all, mixed, image, image_t, own, inc, acc, one, two, theta_ref, x_ref,
    grams, solved, turned_ref, schur, tile_ref, inverses, sides, product_ref, below, whole, reduced, scalars,
    send_sem, recv_sem, local_sem,
):
    links = Links(send_sem, recv_sem)
    links.greet((links.x, links.y, links.d, links.mate))
    core, me, near, far, across = links.core, links.me, links.near, links.far, links.across
    send = links.send
    height, wide = site_ref.shape
    width = wide // 2
    left_site = links.chain - core
    kept_left, kept_mid, kept_right = bond_ref[left_site], bond_ref[left_site + 1], bond_ref[left_site + 2]
    half = height // 2
    quarter = half // 2

    parts = 2
    span = width // parts
    held = pltpu.make_async_copy(site_ref, ab.at[core], local_sem.at[0])
    held.start()
    first = send(site_ref.at[pl.ds(0, half)], ab.at[core, pl.ds(0, half)], links.mate)
    second = send(site_ref.at[pl.ds(half, half)], ab.at[core, pl.ds(half, half)], links.mate)

    def s_block(k, i):
        return s_all.at[k, core, i]

    def s_piece(k, i, p):
        return s_all.at[k, core, i, pl.ds(p * half, half)]

    def s_own(k, p):
        return start_ref.at[pl.ds(p * half, half), pl.ds(k * span, span)]

    starts = []
    for k in range(parts):
        whole_own = start_ref.at[:, pl.ds(k * span, span)]
        starts.append(
            dict(
                held=pltpu.make_async_copy(whole_own, s_block(k, me), local_sem.at[1 + k]),
                mate=links.plan(whole_own, s_block(k, me), links.mate),
                x0=links.plan(s_own(k, 0), s_piece(k, me, 0), links.x),
                y1=links.plan(s_own(k, 1), s_piece(k, me, 1), links.y),
                x1=links.plan(s_own(k, 1), s_piece(k, me, 1), links.x),
                y0=links.plan(s_own(k, 0), s_piece(k, me, 0), links.y),
                forward_y=links.plan(s_piece(k, near, 0), s_piece(k, near, 0), links.y),
                forward_x=links.plan(s_piece(k, far, 1), s_piece(k, far, 1), links.x),
                mate_near=links.plan(s_block(k, near), s_block(k, near), links.mate),
                mate_far=links.plan(s_block(k, far), s_block(k, far), links.mate),
                mate_across=links.plan(s_block(k, across), s_block(k, across), links.mate),
            )
        )

    def s_go(k, *names):
        for name in names:
            starts[k][name].start()

    def s_wait(k, *names):
        for name in names:
            starts[k][name].wait_recv()

    def s_forward(k):
        s_wait(k, "x0")
        s_go(k, "forward_y")
        s_wait(k, "y1")
        s_go(k, "forward_x")

    def s_to_mate(k):
        s_wait(k, "x1")
        s_go(k, "mate_near")
        s_wait(k, "y0")
        s_go(k, "mate_far")
        s_wait(k, "forward_y", "forward_x")
        s_go(k, "mate_across")

    def b_piece(i, p):
        return b_all.at[i, core, pl.ds(p * quarter, quarter)]

    def b_own(p):
        return ab.at[1, pl.ds(pl.multiple_of(core * half + p * quarter, quarter), quarter)]

    s_go(0, "x0", "y1", "mate", "held")
    held.wait()
    first.wait_recv()
    b0x = send(b_own(0), b_piece(me, 0), links.x)
    b1y = send(b_own(1), b_piece(me, 1), links.y)
    second.wait_recv()
    b1x = send(b_own(1), b_piece(me, 1), links.x)
    b0y = send(b_own(0), b_piece(me, 0), links.y)

    line = lax.broadcasted_iota(jnp.int32, (height, CHUNK), 0) + me * height
    lane = lax.broadcasted_iota(jnp.int32, (height, CHUNK), 1)

    def mask(c, carry):
        for i in range(2):
            columns = pl.ds(pl.multiple_of(i * width + c * CHUNK, CHUNK), CHUNK)
            keep = (line < kept_left) & (lane + c * CHUNK < kept_mid)
            used[:, columns] = jnp.where(keep, ab[0, :, columns].astype(jnp.float32), 0.0).astype(jnp.bfloat16)
        return carry

    lax.fori_loop(0, width // CHUNK, mask, 0)
    whole[...] = jnp.zeros_like(whole)

    def mix(load, index, fresh):
        def step(c, carry):
            columns = pl.ds(pl.multiple_of(c * CHUNK, CHUNK), CHUNK)
            right = load(columns)
            for i in range(2):
                left = used[:, pl.ds(pl.multiple_of(i * width + index * height, height), height)]
                product = jnp.dot(left, right, preferred_element_type=jnp.float32)
                mixed[i, :, columns] = product if fresh else mixed[i, :, columns] + product
            return carry

        lax.fori_loop(0, wide // CHUNK, step, 0)

    def gathered(i):
        return lambda columns: b_all[i, :, :, columns].reshape(height, CHUNK)

    mix(lambda columns: ab[1, :, columns], me, True)

    s_forward(0)
    b0x.wait_recv()
    bf_y = send(b_piece(near, 0), b_piece(near, 0), links.y)
    relay_b = [send(b_piece(near, 0), b_piece(near, 0), links.mate)]
    b1y.wait_recv()
    bf_x = send(b_piece(far, 1), b_piece(far, 1), links.x)
    relay_b.append(send(b_piece(far, 1), b_piece(far, 1), links.mate))
    s_go(0, "x1", "y0")
    b1x.wait_recv()
    relay_b.append(send(b_piece(near, 1), b_piece(near, 1), links.mate))
    b0y.wait_recv()
    relay_b.append(send(b_piece(far, 0), b_piece(far, 0), links.mate))
    s_go(1, "x0", "y1", "mate", "held")
    for copy in relay_b:
        copy.wait_recv()
    mix(gathered(near), near, False)
    mix(gathered(far), far, False)
    bf_y.wait_recv()
    last_b = [send(b_piece(across, 0), b_piece(across, 0), links.mate)]
    bf_x.wait_recv()
    last_b.append(send(b_piece(across, 1), b_piece(across, 1), links.mate))
    for copy in last_b:
        copy.wait_recv()
    mix(gathered(across), across, False)

    def form(c, carry):
        offset = c * CHUNK
        inside = lane + offset < kept_right
        parts = []
        for i in range(2):
            for j in range(2):
                columns = pl.ds(pl.multiple_of(j * width + offset, CHUNK), CHUNK)
                parts.append(jnp.where(inside, mixed[i, :, columns], 0.0))
        for o in range(2):
            for q in range(2):
                row = 4 * (2 * o + q)
                value = (
                    gate_ref[left_site, row] * parts[0]
                    + gate_ref[left_site, row + 1] * parts[1]
                    + gate_ref[left_site, row + 2] * parts[2]
                    + gate_ref[left_site, row + 3] * parts[3]
                )
                columns = pl.ds(pl.multiple_of(q * width + offset, CHUNK), CHUNK)
                theta_ref[o, :, columns] = value.astype(jnp.bfloat16)
        return carry

    lax.fori_loop(0, width // CHUNK, form, 0)

    def apply(k, q, i, fresh=False):
        def step(c, carry):
            columns = pl.ds(pl.multiple_of(c * CHUNK, CHUNK), CHUNK)
            there = pl.ds(pl.multiple_of(k * span + c * CHUNK, CHUNK), CHUNK)
            rows = pl.ds(pl.multiple_of(q * width + i * height, height), height)
            product = jnp.dot(
                theta_ref[core, :, rows], s_all[k, q, i, :, columns], preferred_element_type=jnp.float32
            )
            image[:, there] = product if fresh else image[:, there] + product
            return carry

        lax.fori_loop(0, span // CHUNK, step, 0)

    def imaged(k):
        starts[k]["held"].wait()
        apply(k, core, me, True)
        for i in (near, far, across):
            apply(k, core, i)
        s_wait(k, "mate")
        apply(k, 1 - core, me)
        for i, name in ((near, "mate_near"), (far, "mate_far"), (across, "mate_across")):
            s_wait(k, name)
            apply(k, 1 - core, i)

        def turn(c, carry):
            columns = pl.ds(pl.multiple_of(k * span + c * CHUNK, CHUNK), CHUNK)
            kept = lane + k * span + c * CHUNK < kept_mid
            image_t[columns, :] = jnp.where(kept, image[:, columns], 0.0).T.astype(jnp.bfloat16)
            return carry

        lax.fori_loop(0, span // CHUNK, turn, 0)

    def term(k, h, i):
        columns = pl.ds(pl.multiple_of(h * width + i * height, height), height)

        def step(c, carry):
            rows = pl.ds(pl.multiple_of(k * span + c * CHUNK, CHUNK), CHUNK)
            own[h, i, rows, :] = jnp.dot(
                image_t[rows, :], theta_ref[core, :, columns], preferred_element_type=jnp.float32
            ).astype(jnp.bfloat16)
            return carry

        lax.fori_loop(0, span // CHUNK, step, 0)

    order = (across, near, far, me)
    sums = [{} for _ in range(parts)]

    def low(k):
        return pl.ds(k * span, span // 2)

    def high(k):
        return pl.ds(k * span + span // 2, span // 2)

    def exchange(k):
        both = pl.ds(k * span, span)
        sums[k]["swaps"] = []
        for i in order:
            term(k, 1 - core, i)
            sums[k]["swaps"].append(send(own.at[1 - core, i, both], inc.at[i, both], links.mate))

    def reduce_first(k):
        both = pl.ds(k * span, span)

        def merge(position):
            i = order[position]
            term(k, core, i)
            sums[k]["swaps"][position].wait_recv()
            acc[i, both] = add(own[core, i, both], inc[i, both]).astype(jnp.bfloat16)

        merge(0)
        sums[k]["x1"] = send(acc.at[across, low(k)], one.at[k, 0, 1], links.x)
        sums[k]["y1"] = send(acc.at[across, high(k)], one.at[k, 1, 1], links.y)
        merge(1)
        sums[k]["x0"] = send(acc.at[near, low(k)], one.at[k, 0, 0], links.x)
        merge(2)
        sums[k]["y0"] = send(acc.at[far, high(k)], one.at[k, 1, 0], links.y)
        merge(3)

    def reduce_second(k):
        sums[k]["x1"].wait_recv()
        two[k, 2] = add(acc[far, low(k)], one[k, 0, 1]).astype(jnp.bfloat16)
        sums[k]["y2"] = send(two.at[k, 2], two.at[k, 0], links.y)
        sums[k]["y1"].wait_recv()
        two[k, 3] = add(acc[near, high(k)], one[k, 1, 1]).astype(jnp.bfloat16)
        sums[k]["x2"] = send(two.at[k, 3], two.at[k, 1], links.x)

    def reduce_last(k, part):
        for name, n, where in (("0", 0, low(k)), ("1", 1, high(k))):
            sums[k][("x0", "y0")[n]].wait_recv()
            sums[k][("y2", "x2")[n]].wait_recv()
            value = add(acc[me, where], one[k, n, 0]) + two[k, n].astype(jnp.float32)
            value = value.astype(jnp.bfloat16)
            x_ref[core, me, where] = value
            value = value.astype(jnp.float32)
            value = jnp.sum((value * value).reshape(span // 2 // SUB, SUB, height), axis=0)
            for j in range(height // BLOCK):
                part = part + value[:, j * BLOCK : (j + 1) * BLOCK]
        return part

    s_to_mate(0)
    imaged(0)
    s_forward(1)
    s_go(1, "x1", "y0")
    exchange(0)
    reduce_first(0)
    s_to_mate(1)
    reduce_second(0)
    imaged(1)
    exchange(1)
    reduce_first(1)
    part = reduce_last(0, jnp.zeros((SUB, BLOCK), jnp.float32))
    reduce_second(1)

    def piece(i, c, p):
        return x_ref.at[core, i, pl.ds(c * CHUNK + p * BLOCK, BLOCK)]

    def chunk_of(i, c):
        return x_ref.at[core, i, pl.ds(c * CHUNK, CHUNK)]

    chunks = width // CHUNK
    plans = []
    for c in range(chunks):
        plans.append(
            dict(
                y0=links.plan(piece(me, c, 0), piece(me, c, 0), links.y),
                x1=links.plan(piece(me, c, 1), piece(me, c, 1), links.x),
                x0=links.plan(piece(me, c, 0), piece(me, c, 0), links.x),
                y1=links.plan(piece(me, c, 1), piece(me, c, 1), links.y),
                mate=links.plan(chunk_of(me, c), chunk_of(me, c), links.mate),
                forward_x=links.plan(piece(far, c, 0), piece(far, c, 0), links.x),
                forward_y=links.plan(piece(near, c, 1), piece(near, c, 1), links.y),
                mate_near=links.plan(chunk_of(near, c), chunk_of(near, c), links.mate),
                mate_far=links.plan(chunk_of(far, c), chunk_of(far, c), links.mate),
                mate_across=links.plan(chunk_of(across, c), chunk_of(across, c), links.mate),
            )
        )

    def offer(c):
        for name in ("y0", "x1", "x0", "y1", "mate"):
            plans[c][name].start()

    def pass_on(c):
        plans[c]["y0"].wait_recv()
        plans[c]["forward_x"].start()
        plans[c]["x1"].wait_recv()
        plans[c]["forward_y"].start()

    def to_mate(c):
        plans[c]["x0"].wait_recv()
        plans[c]["mate_near"].start()
        plans[c]["y1"].wait_recv()
        plans[c]["mate_far"].start()

    def last_to_mate(c):
        plans[c]["forward_x"].wait_recv()
        plans[c]["forward_y"].wait_recv()
        plans[c]["mate_across"].start()

    def arrive(c):
        for name in ("mate", "mate_near", "mate_far", "mate_across"):
            plans[c][name].wait_recv()

    offer(0)
    part = reduce_last(1, part)

    def spread_sum(value, at, others):
        scalars[at] = value
        copies = [send(scalars.at[at], scalars.at[at + 1 + n], other) for n, other in enumerate(others)]
        for n, copy in enumerate(copies):
            copy.wait_recv()
            value = value + scalars[at + 1 + n]
        return value

    part = spread_sum(part, 0, (links.mate,))
    pass_on(0)
    offer(1)
    part = spread_sum(part, 2, (links.x, links.y, links.d))
    trace = jnp.sum(jnp.sum(part, axis=0, keepdims=True), axis=1, keepdims=True)
    ridge = ridge_ratio * trace / jnp.full((1, 1), kept_mid, jnp.int32).astype(jnp.float32)
    unit, root = 1.0 / ridge, lax.rsqrt(ridge)
    to_mate(0)
    last_to_mate(0)
    arrive(0)

    nt = (((1,), (1,)), ((), ()))
    blocks = [(h, i) for h in range(2) for i in range(width // height)]
    eye = lax.broadcasted_iota(jnp.int32, (CHUNK, CHUNK), 0) == lax.broadcasted_iota(jnp.int32, (CHUNK, CHUNK), 1)
    scalars[6] = jnp.zeros((SUB, BLOCK), jnp.float32)
    inverses[...] = jnp.zeros_like(inverses)
    sides[...] = jnp.zeros_like(sides)

    def upper(c, o, lines):
        reach = (c + 1) * CHUNK
        here = slice(reach - CHUNK, reach)
        value = lax.dot_general(
            jnp.concatenate([reduced[0, lines, :reach], reduced[0, lines, :reach], reduced[1, lines, :reach]], axis=1),
            jnp.concatenate([whole[0, here, :reach], whole[1, here, :reach], whole[0, here, :reach]], axis=1),
            nt, preferred_element_type=jnp.float32,
        )
        out_ref[:, pl.ds(pl.multiple_of(o * width + reach - CHUNK, CHUNK), CHUNK)] = value
        squared = jnp.sum((value * value).reshape(height // SUB, SUB, CHUNK), axis=0)
        part = squared[:, :BLOCK]
        for j in range(1, CHUNK // BLOCK):
            part = part + squared[:, j * BLOCK : (j + 1) * BLOCK]
        scalars[6] = scalars[6] + part

    for c in range(chunks):
        start = c * CHUNK
        reach = start + CHUNK
        here = slice(start, reach)
        for j in range(c + 1):
            value = jnp.zeros((CHUNK, CHUNK), jnp.float32)
            for h, i in blocks:
                value = value + lax.dot_general(
                    x_ref[h, i, j * CHUNK : (j + 1) * CHUNK, :], x_ref[h, i, here, :], nt,
                    preferred_element_type=jnp.float32,
                )
            grams[j * CHUNK : (j + 1) * CHUNK, :] = value
        value = grams[here, :]
        if c > 0:
            for j in range(c):
                to = (j + 1) * CHUNK
                row = slice(j * CHUNK, to)
                solved[row, :] = jnp.dot(
                    jnp.concatenate([whole[0, row, :to], whole[0, row, :to], whole[1, row, :to]], axis=1),
                    threefold(grams[:to, :]),
                    preferred_element_type=jnp.float32,
                )
            turned_ref[:, : 3 * start] = threewide(solved[:start, :].T)
            value = value - jnp.dot(
                turned_ref[:, : 3 * start], threefold(solved[:start, :]), preferred_element_type=jnp.float32
            )
        schur[...] = value + jnp.where(eye, ridge, 0.0)
        tile_ref[...] = unit * schur[:BLOCK, :BLOCK]

        def panel(p, carry, c=c, start=start):
            lines = pl.ds(pl.multiple_of(p * BLOCK, BLOCK), BLOCK)
            columns = pl.ds(pl.multiple_of(start + p * BLOCK, BLOCK), BLOCK)
            inverse = diagonal_inverse(tile_ref[...]) * root
            value = jnp.zeros((2 * height, BLOCK), jnp.float32)
            for h, i in blocks:
                at = h * width + i * height
                value = value + lax.dot_general(
                    theta_ref[:, :, at : at + height].reshape(2 * height, height), x_ref[h, i, columns, :], nt,
                    preferred_element_type=jnp.float32,
                )
            top, low_part = halves(value)
            reduced[0, :, columns] = top
            reduced[1, :, columns] = low_part
            if c > 0:
                product_ref[lines, :start] = jnp.dot(
                    turned_ref[lines, : 3 * start],
                    jnp.concatenate([whole[0, :start, :start], whole[1, :start, :start], whole[0, :start, :start]], axis=0),
                    preferred_element_type=jnp.float32,
                )
            if c > 0:
                upper(c - 1, p, pl.ds(pl.multiple_of(p * height, height), height))
            below[...] = jnp.dot(threewide(sides[...].T), threefold(inverses[0]), preferred_element_type=jnp.float32)
            inverses[p] = inverse

            @pl.when(p == 0)
            def _():
                side = jnp.dot(threewide(inverses[0]), threefold(schur[:BLOCK, BLOCK:]), preferred_element_type=jnp.float32)
                sides[...] = side
                tile_ref[...] = unit * (
                    schur[BLOCK:, BLOCK:]
                    - jnp.dot(threewide(side.T), threefold(side), preferred_element_type=jnp.float32)
                )
                if c + 1 < chunks:
                    to_mate(c + 1)
                    last_to_mate(c + 1)

            return carry

        if c + 1 < chunks:
            pass_on(c + 1)
        if c + 2 < chunks:
            offer(c + 2)
        lax.fori_loop(0, CHUNK // BLOCK, panel, 0)
        if c + 1 < chunks:
            arrive(c + 1)
        corner = -jnp.dot(threewide(inverses[1]), threefold(below[...]), preferred_element_type=jnp.float32)
        own_inverse = jnp.concatenate(
            [
                jnp.concatenate([inverses[0], jnp.zeros((BLOCK, BLOCK), jnp.float32)], axis=1),
                jnp.concatenate([corner, inverses[1]], axis=1),
            ],
            axis=0,
        )
        top, low_part = halves(own_inverse)
        whole[0, here, here] = top
        whole[1, here, here] = low_part
        if c > 0:
            lead = -jnp.dot(
                jnp.concatenate([top, top, low_part], axis=1), threefold(product_ref[:, :start]),
                preferred_element_type=jnp.float32,
            )
            top, low_part = halves(lead)
            whole[0, here, :start] = top
            whole[1, here, :start] = low_part

    @pl.when(core == 0)
    def _():
        for o in range(2):
            upper(chunks - 1, o, slice(o * height, (o + 1) * height))

    @pl.when(core == 1)
    def _():
        rows = pl.ds(pl.multiple_of(me * height, height), height)
        for h, i in blocks:
            at = h * width + i * height
            out_ref[:, at : at + height] = jnp.dot(
                whole[0, rows, :], x_ref[h, i], preferred_element_type=jnp.float32
            ) + jnp.dot(whole[1, rows, :], x_ref[h, i], preferred_element_type=jnp.float32)

    total = spread_sum(scalars[6], 7, (links.x, links.y, links.d))
    total = jnp.sum(jnp.sum(total, axis=0, keepdims=True), axis=1, keepdims=True)

    def real(value):
        return jnp.full((1, 1), value, jnp.int32).astype(jnp.float32)

    mean_square = total / (2.0 * real(kept_left) * real(kept_mid)) + 1e-06
    factor = jnp.where(core == 0, lax.rsqrt(mean_square), jnp.sqrt(2.0 * real(kept_right)))
    factor_ref[...] = factor
    links.drain()


def pair_step(gates, bonds, own_site, own_start):
    rows, wide = own_site.shape
    width = wide // 2
    n = lax.axis_size("bond")
    kind = jnp.bfloat16
    copies = 112
    return pl.pallas_call(
        pair_kernel,
        out_shape=(
            jax.ShapeDtypeStruct((rows, wide), jnp.float32),
            jax.ShapeDtypeStruct((1, 1), jnp.float32),
        ),
        in_specs=[pl.BlockSpec(memory_space=pltpu.SMEM)] * 2 + [pl.BlockSpec(memory_space=pltpu.HBM)] * 2,
        out_specs=(pl.BlockSpec(memory_space=pltpu.VMEM),) * 2,
        scratch_shapes=[
            pltpu.VMEM((2, rows, wide), kind),
            pltpu.VMEM((rows, wide), kind),
            pltpu.VMEM((n, 2, rows // 2, wide), kind),
            pltpu.VMEM((2, 2, n, rows, width // 2), kind),
            pltpu.VMEM((2, rows, wide), jnp.float32),
            pltpu.VMEM((rows, width), jnp.float32),
            pltpu.VMEM((width, rows), kind),
            pltpu.VMEM((2, n, width, rows), kind),
            pltpu.VMEM((n, width, rows), kind),
            pltpu.VMEM((n, width, rows), kind),
            pltpu.VMEM((2, 2, 2, width // 4, rows), kind),
            pltpu.VMEM((2, 4, width // 4, rows), kind),
            pltpu.VMEM((2, rows, wide), kind),
            pltpu.VMEM((2, n, width, rows), kind),
            pltpu.VMEM((width, CHUNK), jnp.float32),
            pltpu.VMEM((width, CHUNK), jnp.float32),
            pltpu.VMEM((CHUNK, 3 * width), kind),
            pltpu.VMEM((CHUNK, CHUNK), jnp.float32),
            pltpu.VMEM((BLOCK, BLOCK), jnp.float32),
            pltpu.VMEM((2, BLOCK, BLOCK), jnp.float32),
            pltpu.VMEM((BLOCK, BLOCK), jnp.float32),
            pltpu.VMEM((CHUNK, width), jnp.float32),
            pltpu.VMEM((BLOCK, BLOCK), jnp.float32),
            pltpu.VMEM((2, width, width), kind),
            pltpu.VMEM((2, 2 * rows, width), kind),
            pltpu.VMEM((11, SUB, BLOCK), jnp.float32),
            pltpu.SemaphoreType.DMA((copies,)),
            pltpu.SemaphoreType.DMA((copies,)),
            pltpu.SemaphoreType.DMA((3,)),
        ],
        compiler_params=pltpu.CompilerParams(
            collective_id=0, has_side_effects=True, vmem_limit_bytes=49 * 1024 * 1024
        ),
    )(gates, bonds, own_site, own_start)


def scaled(rows, sum_squares, bond_left, bond_mid, bond_right, is_left):
    mean_square = (
        sum_squares / (2.0 * bond_left.astype(jnp.float32) * bond_mid.astype(jnp.float32)) + 1e-06
    )
    factor = jnp.where(
        jnp.full(jnp.shape(mean_square), is_left), lax.rsqrt(mean_square), jnp.sqrt(2.0 * bond_right.astype(jnp.float32))
    )
    return (rows * factor)[None]


def local(sites, start, gates, bonds):
    if lax.axis_size("bond") == 4:
        held = [pltpu.with_memory_space_constraint(x, pltpu.HBM) for x in (gates, bonds, sites[0], start[0])]
        rows, factor = pair_step(*held)
        return (rows * factor)[None]
    return spread_out(sites, start, gates, bonds)


def spread_out(sites, start, gates, bonds):
    bond_index = lax.axis_index("bond")
    chain_index = lax.axis_index("chain")
    is_left = chain_index % 2 == 0
    left_site = jnp.where(is_left, chain_index, chain_index - 1)
    rank_width = start.shape[2]
    local_rows = sites.shape[1]
    own_site = sites[0]
    own_start = start[0]
    bond_left = bonds[left_site]
    bond_mid = bonds[left_site + 1]
    bond_right = bonds[left_site + 2]
    bounds = jnp.stack([bond_right, bond_mid, jnp.where(is_left, 0, 1)]).astype(jnp.int32)
    columns = jnp.arange(rank_width)
    row_global = bond_index * local_rows + jnp.arange(local_rows)
    mid_keep = columns < bond_mid
    other_rows = partner(own_site, "chain", 0)
    a_rows = jnp.where(is_left, own_site, other_rows)
    b_rows = jnp.where(is_left, other_rows, own_site)
    b_full = lax.all_gather(b_rows, "bond", axis=0, tiled=True)
    whole_start = lax.all_gather(own_start, "bond", axis=0, tiled=True)
    other_start = partner(whole_start, "chain", 0)
    starts = jnp.stack(
        [jnp.where(is_left, whole_start, other_start), jnp.where(is_left, other_start, whole_start)]
    )
    left_keep = (row_global < bond_left)[:, None] & jnp.tile(mid_keep, 2)[None, :]
    left_used = jnp.where(left_keep, a_rows, jnp.zeros((), jnp.bfloat16))
    thetas, own = theta_terms(gates[left_site], bounds, left_used, b_full, starts)
    kept_half = jnp.where(is_left, 0, 1)
    half_rows = own.shape[0] // 2
    kept = lax.dynamic_slice_in_dim(own, kept_half * half_rows, half_rows, 0)
    given = lax.dynamic_slice_in_dim(own, (1 - kept_half) * half_rows, half_rows, 0)
    both = (kept.astype(jnp.float32) + partner(given, "chain", 0).astype(jnp.float32)).astype(jnp.bfloat16)
    summed = lax.psum_scatter(both, "bond", scatter_dimension=0, tiled=True)
    own_half = lax.all_gather(summed, "bond", axis=0, tiled=True)
    other_half = partner(own_half, "chain", 0)
    projected_all = jnp.concatenate(
        [jnp.where(is_left, own_half, other_half), jnp.where(is_left, other_half, own_half)], axis=0
    )
    gram = lax.dot_general(
        projected_all, projected_all, (((0,), (0,)), ((), ())), preferred_element_type=jnp.float32
    )
    inverse = factor_inverse(bounds, gram)

    def left_rows():
        reduced = jnp.dot(
            thetas.reshape(2 * local_rows, -1), projected_all, preferred_element_type=jnp.float32
        )
        upper = lax.dot_general(
            reduced,
            inverse,
            (((1,), (1,)), ((), ())),
            precision=lax.Precision.HIGH,
            preferred_element_type=jnp.float32,
        )
        joined = jnp.concatenate([upper[:local_rows], upper[local_rows:]], axis=1)
        return joined, jnp.sum(joined * joined)

    def right_rows():
        block = lax.dynamic_slice_in_dim(inverse, bond_index * local_rows, local_rows, 0)
        basis_rows = lax.dot_general(
            block,
            projected_all.astype(jnp.float32),
            (((1,), (1,)), ((), ())),
            precision=lax.Precision.HIGH,
            preferred_element_type=jnp.float32,
        )
        return basis_rows, jnp.float32(0.0)

    rows, squares = lax.cond(is_left, left_rows, right_rows)
    return scaled(rows, lax.psum(squares, "bond"), bond_left, bond_mid, bond_right, is_left)


def solution(mesh):
    placed = (P("chain", "bond", None), P("chain", "bond", None), P(), P())
    return jax.shard_map(
        local, mesh=mesh, in_specs=placed, out_specs=P("chain", "bond", None), check_vma=False
    )
```
